256 devices in a mesh: src: 64 (over y, z, core), tgt: 4 (over x).
Axes of the slice: x: 4, y: 4, z: 8, core: 2. Of those that a mesh axis runs over, the one named last changes fastest.
Arguments:
- text_emb: bfloat16 [131072, 512], P('src'), may hold values from -32 to 32
- image_emb: bfloat16 [8192, 512], P('tgt'), may hold values from -12 to 12
- log_mass_src: float32 [131072], P('src'), may hold values from -1 to 1
- log_mass_tgt: float32 [8192], P('tgt'), may hold values from -1 to 1
- pair_blocks: int32 [4096, 2], P(('src', 'tgt')), may hold values from 0 to 7, as said below
- pair_counts: int32 [256], P(('src', 'tgt')), may hold values from 2 to 16, as said below
Outputs:
- src_map: float32 [131072, 512], P(('src', 'tgt'))
- tgt_map: float32 [8192, 512], P(('tgt', 'src'))
The draws below stay inside these ranges and needn't reach their ends.
Inputs may be any that keep to these rules, and one draw needn't show every extreme that they name: `pair_blocks`: column 0 is a local text cluster below 8, column 1 a local image cluster below 8. The first pair_counts slots of a device hold distinct pairs; every text cluster and every image cluster lies in some used slot. Unused slots hold valid indices that are ignored. `pair_counts`: at least 8 // 4 used slots on every device; some device uses all 16 in every draw.
All inputs are finite; a program needn't handle non-finite values.
Results may differ from the reference program's by a relative error of at most 0.0028.
Values sent between devices are 32-bit elements; how exact they have to be, the bound alone decides.
No kernel may reach another device: no remote copies, remote signals or barrier semaphores. Data moves between devices by JAX's collectives and lax.ppermute only.
A program may use at most 64 MiB of HBM per device.

```python
import jax
import jax.numpy as jnp
from jax import lax

D = 512
BLK = 256
SB_DEV = 8
TB_GRP = 8
ITERS = 3
PAIR_CAP = 16
NS = 131072
NT = 8192
N_SRC = 64
N_TGT = 4


def pair_layout(key):
    base = jax.random.fold_in(key, 7)
    ndevices = N_SRC * N_TGT
    each = SB_DEV // N_TGT
    combos = SB_DEV * TB_GRP
    device_ids = jnp.arange(ndevices, dtype=jnp.int32)
    src_index = device_ids // N_TGT
    tgt_index = device_ids % N_TGT
    rank = jnp.arange(each, dtype=jnp.int32)
    sure_src = tgt_index[:, None] + N_TGT * rank[None, :]
    sure_tgt = (src_index[:, None] * each + rank[None, :]) % TB_GRP
    sure_combo = sure_src * TB_GRP + sure_tgt
    noise = jax.random.randint(jax.random.fold_in(base, 1), (ndevices, combos), 0, 1 << 20)
    combo_ids = jnp.arange(combos, dtype=jnp.int32)
    score = noise * combos + combo_ids[None, :]
    hit = (combo_ids[None, None, :] == sure_combo[:, :, None]).any(axis=1)
    score = score + jnp.where(hit, 1 << 30, 0)
    _, chosen = lax.top_k(score, PAIR_CAP)
    draws = jax.random.randint(jax.random.fold_in(base, 2), (ndevices,), 0, PAIR_CAP)
    extra = jnp.minimum(draws * draws // (PAIR_CAP - 2), PAIR_CAP - each)
    counts = each + extra
    busiest = jax.random.randint(jax.random.fold_in(base, 3), (), 0, ndevices)
    counts = jnp.where(device_ids == busiest, PAIR_CAP, counts)
    blocks = jnp.stack([chosen // TB_GRP, chosen % TB_GRP], axis=-1).reshape(ndevices * PAIR_CAP, 2)
    return (blocks.astype(jnp.int32), counts.astype(jnp.int32))


def draw_pair_blocks(key, part):
    return pair_layout(key)[0]


def draw_pair_counts(key, part):
    return pair_layout(key)[1]


def draw_text_emb(key, part):
    rows = SB_DEV * BLK * N_SRC
    values = jax.random.truncated_normal(jax.random.fold_in(key, 5), -4.0, 4.0, (rows, D), jnp.float32)
    return values.astype(jnp.bfloat16)


def draw_image_emb(key, part):
    rows = TB_GRP * BLK * N_TGT
    values = jax.random.truncated_normal(jax.random.fold_in(key, 9), -4.0, 4.0, (rows, D), jnp.float32)
    return values.astype(jnp.bfloat16)


def shard_levels(key, extent, shards, least, top_value):
    level, own = 1.0, jax.random.fold_in(key, 6)
    for position, blocks in shards:
        steps = jnp.exp(jax.random.uniform(jax.random.fold_in(own, position), (blocks,), jnp.float32, least / len(shards), top_value / len(shards)))
        level = level * jnp.repeat(steps, extent[position] // blocks).reshape([-1 if axis == position else 1 for axis in range(len(extent))])
    return level


def setup_inputs(seed: int = 0) -> dict:
    streams_of = jax.random.split(jax.random.key(seed), 7)
    text_emb = draw_text_emb(jax.random.fold_in(streams_of[6], 71), 0)
    image_emb = draw_image_emb(jax.random.fold_in(streams_of[6], 71), 0)
    log_mass_src = jnp.clip(jax.random.uniform(streams_of[2], (NS,), jnp.float32, -1.0, 1.0) * shard_levels(streams_of[2], (NS,), ((0, 64),), -0.4, 0.0), -1.0, 1.0)
    log_mass_tgt = jnp.clip(jax.random.uniform(streams_of[3], (NT,), jnp.float32, -1.0, 1.0) * shard_levels(streams_of[3], (NT,), ((0, 4),), -0.4, 0.0), -1.0, 1.0)
    pair_blocks = draw_pair_blocks(jax.random.fold_in(streams_of[6], 71), 0)
    pair_counts = draw_pair_counts(jax.random.fold_in(streams_of[6], 71), 0)
    return dict(text_emb=text_emb, image_emb=image_emb, log_mass_src=log_mass_src, log_mass_tgt=log_mass_tgt, pair_blocks=pair_blocks, pair_counts=pair_counts)


inv_temp = 0.15
floor_value = -1e30


def reference(text_emb, image_emb, log_mass_src, log_mass_tgt, pair_blocks, pair_counts):
    total = N_SRC * N_TGT * PAIR_CAP
    slot_ids = jnp.arange(total, dtype=jnp.int32)
    device_ids = slot_ids // PAIR_CAP
    valid = (slot_ids % PAIR_CAP) < pair_counts[device_ids]
    src_blk = ((device_ids // N_TGT) * SB_DEV + pair_blocks[:, 0]).astype(jnp.int32)
    tgt_blk = ((device_ids % N_TGT) * TB_GRP + pair_blocks[:, 1]).astype(jnp.int32)
    src_count = SB_DEV * N_SRC
    tgt_count = TB_GRP * N_TGT
    text_blocks = text_emb.reshape(src_count, BLK, D)
    image_blocks = image_emb.reshape(tgt_count, BLK, D)

    def score_tile(index):
        return jnp.dot(text_blocks[index[0]], image_blocks[index[1]].T, preferred_element_type=jnp.float32) * inv_temp

    tiles = lax.map(score_tile, (src_blk, tgt_blk))
    mask = valid[:, None, None]
    mass_src = log_mass_src.reshape(src_count, BLK)
    mass_tgt = log_mass_tgt.reshape(tgt_count, BLK)
    tgt_pot = jnp.zeros((tgt_count, BLK), jnp.float32)
    src_pot = jnp.zeros((src_count, BLK), jnp.float32)
    for step in range(ITERS):
        shifted = jnp.where(mask, tiles + tgt_pot[tgt_blk][:, None, :], floor_value)
        peak = jnp.full((src_count, BLK), floor_value, jnp.float32).at[src_blk].max(shifted.max(axis=2))
        sums = jnp.zeros((src_count, BLK), jnp.float32).at[src_blk].add(
            jnp.exp(shifted - peak[src_blk][:, :, None]).sum(axis=2))
        src_pot = mass_src - peak - jnp.log(sums)
        shifted = jnp.where(mask, tiles + src_pot[src_blk][:, :, None], floor_value)
        peak = jnp.full((tgt_count, BLK), floor_value, jnp.float32).at[tgt_blk].max(shifted.max(axis=1))
        sums = jnp.zeros((tgt_count, BLK), jnp.float32).at[tgt_blk].add(
            jnp.exp(shifted - peak[tgt_blk][:, None, :]).sum(axis=1))
        tgt_pot = mass_tgt - peak - jnp.log(sums)
    plan = jnp.where(mask, jnp.exp(tiles + src_pot[src_blk][:, :, None] + tgt_pot[tgt_blk][:, None, :]), 0.0)
    row_mass = jnp.zeros((src_count, BLK), jnp.float32).at[src_blk].add(plan.sum(axis=2))
    col_mass = jnp.zeros((tgt_count, BLK), jnp.float32).at[tgt_blk].add(plan.sum(axis=1))
    weights = plan.astype(jnp.bfloat16)

    def accumulate(carry, item):
        src_numer, tgt_numer = carry
        weight, src_index, tgt_index = item
        src_numer = src_numer.at[src_index].add(
            jnp.dot(weight, image_blocks[tgt_index], preferred_element_type=jnp.float32))
        tgt_numer = tgt_numer.at[tgt_index].add(
            jnp.dot(weight.T, text_blocks[src_index], preferred_element_type=jnp.float32))
        return (src_numer, tgt_numer), None

    start = (jnp.zeros((src_count, BLK, D), jnp.float32), jnp.zeros((tgt_count, BLK, D), jnp.float32))
    (src_numer, tgt_numer), _ = lax.scan(accumulate, start, (weights, src_blk, tgt_blk))
    src_map = (src_numer / row_mass[:, :, None]).reshape(NS, D)
    tgt_map = (tgt_numer / col_mass[:, :, None]).reshape(NT, D)
    return (src_map, tgt_map)
```

```python
import functools

import jax
import jax.numpy as jnp
from jax import lax
from jax.experimental import pallas as pl
from jax.experimental.pallas import tpu as pltpu
from jax.sharding import Mesh, PartitionSpec as P

BLK = 256
ITERS = 3
NB = 8
CAP = 16
D = 512
NX, NY, NZ, NC = 4, 4, 8, 2
FLOOR = -1e30
INV_TEMP = 0.15
STEP = 64


VMEM = pl.BlockSpec(memory_space=pltpu.VMEM)
SMEM = pl.BlockSpec(memory_space=pltpu.SMEM)
f32 = jnp.float32


def lse_of(parts):
    peak = functools.reduce(jnp.maximum, parts)
    total = sum(jnp.exp(p - peak) for p in parts)
    return peak + jnp.log(total)


def lse_stack(ref):
    peak = jnp.max(ref[...], axis=0)
    total = jnp.sum(jnp.exp(ref[...] - peak[None]), axis=0)
    return peak + jnp.log(total)


def slots(cnt, pairs, body):
    def step(k, _):
        body(k, pairs[k, 0], pairs[k, 1])
        return 0

    lax.fori_loop(0, cnt[0], step, 0)


def to_columns(rows):
    padded = jnp.concatenate([rows, jnp.zeros((120, BLK), f32)], axis=0)
    return jnp.transpose(padded)


def spread_columns(rows, out):
    cols = to_columns(rows)
    for a in range(NB):
        out[a] = jnp.broadcast_to(cols[:, a : a + 1], (BLK, 128))


def columns_to_rows(columns):
    lane = lax.broadcasted_iota(jnp.int32, (BLK, 128), 1)
    table = jnp.zeros((BLK, 128), f32)
    for a in range(NB):
        table = jnp.where(lane == a, columns[a], table)
    return jnp.transpose(table)[:NB]


def row_totals(cnt, pairs, scores, v, m_ref, s_ref, lse_out):
    for a in range(NB):
        m_ref[a] = jnp.broadcast_to(jnp.max(m_ref[a], axis=1, keepdims=True), (BLK, 128))
        s_ref[a] = jnp.zeros((BLK, 128), f32)

    def body(k, a, b):
        shift = v[pl.ds(b, 1), :] if v is not None else None
        for r in range(0, BLK, STEP):
            rows = slice(r, r + STEP)
            tile = scores[k, rows, :]
            if shift is not None:
                tile = tile + shift
            peak = m_ref[a, rows, :]
            s_ref[a, rows, :] += jnp.exp(tile[:, :128] - peak) + jnp.exp(tile[:, 128:] - peak)

    slots(cnt, pairs, body)
    columns = []
    for a in range(NB):
        total = jnp.sum(s_ref[a], axis=1, keepdims=True)
        value = jnp.where(total > 0, m_ref[a, :, :1] + jnp.log(total), FLOOR)
        columns.append(jnp.broadcast_to(value, (BLK, 128)))
    lse_out[...] = columns_to_rows(columns)


def first_kernel(cnt, pairs, text, image, scores, lse_out, m_ref, s_ref):
    m_ref[...] = jnp.full(m_ref.shape, FLOOR, f32)

    def body(k, a, b):
        tile = (
            lax.dot_general(
                text[pl.ds(pl.multiple_of(a * BLK, BLK), BLK), :],
                image[pl.ds(pl.multiple_of(b * BLK, BLK), BLK), :],
                (((1,), (1,)), ((), ())),
                preferred_element_type=f32,
            )
            * INV_TEMP
        )
        scores[k] = tile
        m_ref[a] = jnp.maximum(m_ref[a], jnp.maximum(tile[:, :128], tile[:, 128:]))

    slots(cnt, pairs, body)
    row_totals(cnt, pairs, scores, None, m_ref, s_ref, lse_out)


def row_kernel(cnt, pairs, scores, parts, mass, lse_out, v_ref, m_ref, s_ref):
    v_ref[...] = mass[...] - lse_stack(parts)
    m_ref[...] = jnp.full(m_ref.shape, FLOOR, f32)

    def body(k, a, b):
        shift = v_ref[pl.ds(b, 1), :]
        for r in range(0, BLK, STEP):
            rows = slice(r, r + STEP)
            tile = scores[k, rows, :] + shift
            m_ref[a, rows, :] = jnp.maximum(
                m_ref[a, rows, :], jnp.maximum(tile[:, :128], tile[:, 128:])
            )

    slots(cnt, pairs, body)
    row_totals(cnt, pairs, scores, v_ref, m_ref, s_ref, lse_out)


def col_kernel(cnt, pairs, scores, p0, p1, p2, p3, mass, lse_out, u_out, u_ref, m_ref, s_ref):
    u = mass[...] - lse_of([p0[...], p1[...], p2[...], p3[...]])
    u_out[...] = u
    spread_columns(u, u_ref)
    m_ref[...] = jnp.full(m_ref.shape, FLOOR, f32)
    s_ref[...] = jnp.zeros(s_ref.shape, f32)

    def shifted(k, a, r, half):
        tile = scores[k, r : r + STEP, half * 128 : half * 128 + 128] + u_ref[a, r : r + STEP, :]
        return tile.reshape(STEP // 8, 8, 128)

    def peaks(k, a, b):
        for half in range(2):
            lanes = slice(half * 128, half * 128 + 128)
            best = m_ref[b, :, lanes]
            for r in range(0, BLK, STEP):
                best = jnp.maximum(best, jnp.max(shifted(k, a, r, half), axis=0))
            m_ref[b, :, lanes] = best

    slots(cnt, pairs, peaks)
    for b in range(NB):
        m_ref[b] = jnp.broadcast_to(jnp.max(m_ref[b], axis=0, keepdims=True), (8, BLK))

    def totals(k, a, b):
        for half in range(2):
            lanes = slice(half * 128, half * 128 + 128)
            peak = m_ref[b, :, lanes]
            total = s_ref[b, :, lanes]
            for r in range(0, BLK, STEP):
                total = total + jnp.sum(jnp.exp(shifted(k, a, r, half) - peak[None]), axis=0)
            s_ref[b, :, lanes] = total

    slots(cnt, pairs, totals)
    for b in range(NB):
        total = jnp.sum(s_ref[b], axis=0, keepdims=True)
        lse_out[b : b + 1, :] = jnp.where(total > 0, m_ref[b, :1, :] + jnp.log(total), FLOOR)


def final_kernel(
    cnt, pairs, place, scores, parts, mass, u, text, image, *refs
):
    src_out = refs[:8]
    keep, send = refs[8:10]
    v_ref, u_ref, w_ref, src_acc, tgt_acc, rsum, csum, rmass = refs[10:]
    v_ref[...] = mass[...] - lse_stack(parts)
    spread_columns(u[...], u_ref)
    src_acc[...] = jnp.zeros(src_acc.shape, f32)
    tgt_acc[...] = jnp.zeros(tgt_acc.shape, f32)
    rsum[...] = jnp.zeros(rsum.shape, f32)
    csum[...] = jnp.zeros(csum.shape, f32)

    def body(k, a, b):
        v = v_ref[pl.ds(b, 1), :]
        for r in range(0, BLK, STEP):
            rows = slice(r, r + STEP)
            for half in range(2):
                lanes = slice(half * 128, half * 128 + 128)
                plan = jnp.exp(
                    scores[k, rows, lanes] + u_ref[a, rows, :] + v[:, lanes]
                )
                rsum[a, rows, :] += plan
                csum[b, :, lanes] += jnp.sum(plan.reshape(STEP // 8, 8, 128), axis=0)
                w_ref[rows, lanes] = plan.astype(jnp.bfloat16)
        weight = w_ref[...]
        src_acc[a] += jnp.dot(
            weight,
            image[pl.ds(pl.multiple_of(b * BLK, BLK), BLK), :],
            preferred_element_type=f32,
        )
        tgt_acc[b] += lax.dot_general(
            weight,
            text[pl.ds(pl.multiple_of(a * BLK, BLK), BLK), :],
            (((0,), (0,)), ((), ())),
            preferred_element_type=f32,
        )

    slots(cnt, pairs, body)
    rmass[...] = columns_to_rows(
        [
            jnp.broadcast_to(jnp.sum(rsum[a], axis=1, keepdims=True), (BLK, 128))
            for a in range(NB)
        ]
    )
    x, y, c = place[0], place[1], place[2]
    for r in range(NB):
        a = lax.rem(2 * x + r, NB)
        src_out[r][:BLK, :] = src_acc[a]
        src_out[r][BLK:, :BLK] = jnp.broadcast_to(rmass[pl.ds(a, 1), :], (8, BLK))
        src_out[r][BLK:, BLK:] = jnp.zeros((8, D - BLK), f32)
    cols = jnp.concatenate(
        [jnp.sum(csum[b], axis=0, keepdims=True) for b in range(NB)], axis=0
    )
    spread_columns(cols, u_ref)
    lane = lax.broadcasted_iota(jnp.int32, (8, 128), 1)
    for r in range(NY):
        b0 = 2 * lax.rem(y + r, NY)
        for z in range(NZ):
            b = b0 + z // 4
            for out, core in ((keep, c), (send, 1 - c)):
                base = pl.multiple_of((z % 4) * 64 + core * 32, 32)
                block = jnp.zeros((8, 128), f32)
                for g in range(4):
                    out[r, z, :, g * D : g * D + D] = tgt_acc[b, pl.ds(base + 8 * g, 8), :]
                    block = jnp.where(lane == g, u_ref[b, pl.ds(base + 8 * g, 8), :], block)
                out[r, z, :, 4 * D :] = block


def src_norm_kernel(own, plus, minus, out):
    total = own[...] + plus[...] + minus[...]
    cols = to_columns(total[BLK:, :BLK])
    out[...] = total[:BLK, :] / cols[:, :1]


def tgt_norm_kernel(parts, out):
    total = jnp.sum(parts[...], axis=0)
    for g in range(4):
        column = total[:, 4 * D + g : 4 * D + g + 1]
        out[8 * g : 8 * g + 8, :] = total[:, g * D : g * D + D] / column


def call(kernel, outs, args, smem, scratch=(), name=None):
    return pl.pallas_call(
        kernel,
        out_shape=outs,
        in_specs=[SMEM] * smem + [VMEM] * (len(args) - smem),
        out_specs=jax.tree.map(lambda _: VMEM, outs),
        scratch_shapes=list(scratch),
        compiler_params=pltpu.CompilerParams(vmem_limit_bytes=56 << 20),
        name=name,
    )(*args)


def sds(*shape):
    return jax.ShapeDtypeStruct(shape, f32)


def shift(a, axis, size, by):
    return lax.ppermute(a, axis, [(i, (i + by) % size) for i in range(size)])


def over_x(part):
    return [part] + [shift(part, "x", NX, k) for k in (1, 3, 2)]


def over_src(part):
    other = shift(part, "c", NC, 1)
    both = lse_of([part, other])
    copies = jnp.broadcast_to(both[None], (NY * NZ, NB, BLK))
    return lax.all_to_all(copies, ("y", "z"), 0, 0, tiled=True)


def ring_scatter(own_a, own_b, plus_a, plus_b, far_a, far_b, minus_a, minus_b, axis, size):
    relay_up = shift(far_a, axis, size, 1)
    relay_down = shift(far_b, axis, size, -1)
    from_below_b = shift(plus_b, axis, size, 1)
    from_above_a = shift(minus_a, axis, size, -1)
    from_below_a = shift(plus_a + relay_up, axis, size, 1)
    from_above_b = shift(minus_b + relay_down, axis, size, -1)
    return (own_a, from_below_a, from_above_a), (own_b, from_below_b, from_above_b)


def local(text, image, log_mass_src, log_mass_tgt, pairs, count):
    mass_src = log_mass_src.reshape(NB, BLK)
    mass_tgt = log_mass_tgt.reshape(NB, BLK)
    row_scratch = [pltpu.VMEM((NB, BLK, 128), f32)] * 2
    col_scratch = [pltpu.VMEM((NB, BLK, 128), f32)] + [pltpu.VMEM((NB, 8, BLK), f32)] * 2
    scores, part = call(
        first_kernel,
        (sds(CAP, BLK, BLK), sds(NB, BLK)),
        (count, pairs, text, image),
        2,
        row_scratch,
        "first",
    )
    for step in range(ITERS):
        got = over_x(part)
        part, u = call(
            col_kernel,
            (sds(NB, BLK), sds(NB, BLK)),
            (count, pairs, scores, *got, mass_src),
            2,
            col_scratch,
            "cols",
        )
        stack = over_src(part)
        if step < ITERS - 1:
            part = call(
                row_kernel,
                sds(NB, BLK),
                (count, pairs, scores, stack, mass_tgt),
                2,
                [pltpu.VMEM((NB, BLK), f32)] + row_scratch,
                "rows",
            )
    place = jnp.stack([lax.axis_index("x"), lax.axis_index("y"), lax.axis_index("c")])
    piece = sds(NY, NZ, 8, 4 * D + 128)
    outs = call(
        final_kernel,
        tuple([sds(BLK + 8, D)] * 8 + [piece, piece]),
        (count, pairs, place, scores, stack, mass_tgt, u, text, image),
        3,
        [
            pltpu.VMEM((NB, BLK), f32),
            pltpu.VMEM((NB, BLK, 128), f32),
            pltpu.VMEM((BLK, BLK), jnp.bfloat16),
            pltpu.VMEM((NB, BLK, D), f32),
            pltpu.VMEM((NB, BLK, D), f32),
            pltpu.VMEM((NB, BLK, 128), f32),
            pltpu.VMEM((NB, 8, BLK), f32),
            pltpu.VMEM((NB, BLK), f32),
        ],
        "final",
    )
    keep, send = outs[8:]
    part_a, part_b = ring_scatter(*outs[:8], "x", NX)
    both = keep + shift(send, "c", NC, 1)
    halves = [both[r, h : h + 4] for r in range(NY) for h in (0, 4)]
    tgt_a, tgt_b = ring_scatter(*halves, "y", NY)
    summed = jnp.concatenate([sum(tgt_a), sum(tgt_b)], axis=0)
    got = lax.all_to_all(summed, "z", 0, 0, tiled=True)
    tgt_map = call(tgt_norm_kernel, sds(32, D), (got,), 0, (), "tgt_norm")
    src_map = jnp.concatenate(
        [call(src_norm_kernel, sds(BLK, D), p, 0, (), "src_norm") for p in (part_a, part_b)],
        axis=0,
    )
    return (src_map, tgt_map)


def solution(mesh):
    grid = Mesh(mesh.devices.reshape(NY, NZ, NC, NX), ("y", "z", "c", "x"))
    src = ("y", "z", "c")
    return jax.shard_map(
        local,
        mesh=grid,
        in_specs=(P(src, None), P("x", None), P(src), P("x"), P((*src, "x"), None), P((*src, "x"))),
        out_specs=(P((*src, "x"), None), P(("x", *src), None)),
        check_vma=False,
    )
```

```python
import functools

import jax
import jax.numpy as jnp
from jax import lax
from jax.experimental import pallas as pl
from jax.experimental.pallas import tpu as pltpu
from jax.sharding import Mesh, PartitionSpec as P


BLK = 256
ITERS = 3
NB = 8
CAP = 16
D = 512
NX, NY, NZ, NC = 4, 4, 8, 2
FLOOR = -1e30
INV_TEMP = 0.15
STEP = 64


VMEM = pl.BlockSpec(memory_space=pltpu.VMEM)
SMEM = pl.BlockSpec(memory_space=pltpu.SMEM)
HBM = pl.BlockSpec(memory_space=pltpu.HBM)
f32 = jnp.float32


def lse_of(parts):
    peak = functools.reduce(jnp.maximum, parts)
    total = sum(jnp.exp(p - peak) for p in parts)
    return peak + jnp.log(total)


def lse_stack(ref):
    peak = jnp.max(ref[...], axis=0)
    total = jnp.sum(jnp.exp(ref[...] - peak[None]), axis=0)
    return peak + jnp.log(total)


def slots(cnt, pairs, body):
    def step(k, _):
        pair = pairs[k]
        body(k, pair // NB, pair % NB)
        return 0

    lax.fori_loop(0, cnt[0], step, 0)


def every_slot(cnt, act):
    def step(k, _):
        act(k)
        return 0

    lax.fori_loop(0, cnt[0], step, 0)


def fetch_scores(cnt, held, scores, sem):
    every_slot(cnt, lambda k: pltpu.make_async_copy(held.at[k], scores.at[k], sem.at[k]).start())
    return lambda k: pltpu.make_async_copy(held.at[k], scores.at[k], sem.at[k]).wait()


def fetch_blocks(held, out, sem):
    copies = [
        pltpu.make_async_copy(held.at[pl.ds(i * BLK, BLK), :], out.at[i], sem.at[i])
        for i in range(NB)
    ]
    for copy in copies:
        copy.start()
    return copies


def to_columns(rows):
    padded = jnp.concatenate([rows, jnp.zeros((120, BLK), f32)], axis=0)
    return jnp.transpose(padded)


def spread_columns(rows, out):
    cols = to_columns(rows)
    for a in range(NB):
        out[a] = jnp.broadcast_to(cols[:, a : a + 1], (BLK, 128))


def columns_to_rows(columns):
    lane = lax.broadcasted_iota(jnp.int32, (BLK, 128), 1)
    table = jnp.zeros((BLK, 128), f32)
    for a in range(NB):
        table = jnp.where(lane == a, columns[a], table)
    return jnp.transpose(table)[:NB]


def row_totals(cnt, pairs, scores, v, m_ref, s_ref, lse_out):
    for a in range(NB):
        m_ref[a] = jnp.broadcast_to(jnp.max(m_ref[a], axis=1, keepdims=True), (BLK, 128))
        s_ref[a] = jnp.zeros((BLK, 128), f32)

    def body(k, a, b):
        shift = v[pl.ds(b, 1), :] if v is not None else None
        for r in range(0, BLK, STEP):
            rows = slice(r, r + STEP)
            tile = scores[k, rows, :]
            if shift is not None:
                tile = tile + shift
            peak = m_ref[a, rows, :]
            s_ref[a, rows, :] += jnp.exp(tile[:, :128] - peak) + jnp.exp(tile[:, 128:] - peak)

    slots(cnt, pairs, body)
    columns = []
    for a in range(NB):
        total = jnp.sum(s_ref[a], axis=1, keepdims=True)
        value = jnp.where(total > 0, m_ref[a, :, :1] + jnp.log(total), FLOOR)
        columns.append(jnp.broadcast_to(value, (BLK, 128)))
    lse_out[...] = columns_to_rows(columns)


def first_kernel(
    cnt, pairs, text, image, held, lse_out, m_ref, s_ref, scores, texts, images, sem, tsem, isem
):
    copies = fetch_blocks(text, texts, tsem) + fetch_blocks(image, images, isem)
    m_ref[...] = jnp.full(m_ref.shape, FLOOR, f32)
    for copy in copies:
        copy.wait()

    def body(k, a, b):
        tile = (
            lax.dot_general(
                texts[a], images[b], (((1,), (1,)), ((), ())), preferred_element_type=f32
            )
            * INV_TEMP
        )
        scores[k] = tile
        m_ref[a] = jnp.maximum(m_ref[a], jnp.maximum(tile[:, :128], tile[:, 128:]))

    slots(cnt, pairs, body)
    every_slot(cnt, lambda k: pltpu.make_async_copy(scores.at[k], held.at[k], sem.at[k]).start())
    row_totals(cnt, pairs, scores, None, m_ref, s_ref, lse_out)
    every_slot(cnt, lambda k: pltpu.make_async_copy(scores.at[k], held.at[k], sem.at[k]).wait())


def row_kernel(cnt, pairs, held, parts, mass, lse_out, v_ref, m_ref, s_ref, scores, sem):
    arrive = fetch_scores(cnt, held, scores, sem)
    v_ref[...] = mass[...] - lse_stack(parts)
    m_ref[...] = jnp.full(m_ref.shape, FLOOR, f32)

    def body(k, a, b):
        arrive(k)
        shift = v_ref[pl.ds(b, 1), :]
        for r in range(0, BLK, STEP):
            rows = slice(r, r + STEP)
            tile = scores[k, rows, :] + shift
            m_ref[a, rows, :] = jnp.maximum(
                m_ref[a, rows, :], jnp.maximum(tile[:, :128], tile[:, 128:])
            )

    slots(cnt, pairs, body)
    row_totals(cnt, pairs, scores, v_ref, m_ref, s_ref, lse_out)


def col_peaks(cnt, pairs, scores, arrive, u, u_ref, m_ref, s_ref):
    spread_columns(u, u_ref)
    m_ref[...] = jnp.full(m_ref.shape, FLOOR, f32)
    s_ref[...] = jnp.zeros(s_ref.shape, f32)

    def peaks(k, a, b):
        arrive(k)
        for half in range(2):
            lanes = slice(half * 128, half * 128 + 128)
            best = m_ref[b, :, lanes]
            for r in range(0, BLK, STEP):
                tile = scores[k, r : r + STEP, lanes] + u_ref[a, r : r + STEP, :]
                best = jnp.maximum(best, jnp.max(tile.reshape(STEP // 8, 8, 128), axis=0))
            m_ref[b, :, lanes] = best

    slots(cnt, pairs, peaks)
    for b in range(NB):
        m_ref[b] = jnp.broadcast_to(jnp.max(m_ref[b], axis=0, keepdims=True), (8, BLK))


def col_lse(m_ref, s_ref, lse_out):
    totals = []
    for b in range(NB):
        total = jnp.sum(s_ref[b], axis=0, keepdims=True)
        lse_out[b : b + 1, :] = jnp.where(total > 0, m_ref[b, :1, :] + jnp.log(total), FLOOR)
        totals.append(total)
    return totals


def col_kernel(
    cnt, pairs, held, p0, p1, p2, p3, mass, lse_out, u_ref, m_ref, s_ref, scores, sem
):
    arrive = fetch_scores(cnt, held, scores, sem)
    u = mass[...] - lse_of([p0[...], p1[...], p2[...], p3[...]])
    col_peaks(cnt, pairs, scores, arrive, u, u_ref, m_ref, s_ref)

    def totals(k, a, b):
        for half in range(2):
            lanes = slice(half * 128, half * 128 + 128)
            peak = m_ref[b, :, lanes]
            total = s_ref[b, :, lanes]
            for r in range(0, BLK, STEP):
                tile = scores[k, r : r + STEP, lanes] + u_ref[a, r : r + STEP, :]
                tile = jnp.exp(tile.reshape(STEP // 8, 8, 128) - peak[None])
                total = total + jnp.sum(tile, axis=0)
            s_ref[b, :, lanes] = total

    slots(cnt, pairs, totals)
    col_lse(m_ref, s_ref, lse_out)


def last_col_kernel(
    cnt, pairs, place, held, p0, p1, p2, p3, mass, text, lse_out, u_out, keep, send,
    u_ref, m_ref, s_ref, scores, sem, texts, tsem, hi_ref, lo_ref, acc,
):
    arrive = fetch_scores(cnt, held, scores, sem)
    copies = fetch_blocks(text, texts, tsem)
    u = mass[...] - lse_of([p0[...], p1[...], p2[...], p3[...]])
    u_out[...] = u
    col_peaks(cnt, pairs, scores, arrive, u, u_ref, m_ref, s_ref)
    acc[...] = jnp.zeros(acc.shape, f32)
    for copy in copies:
        copy.wait()

    def totals(k, a, b):
        for half in range(2):
            lanes = slice(half * 128, half * 128 + 128)
            peak = m_ref[b, :, lanes]
            total = s_ref[b, :, lanes]
            for r in range(0, BLK, STEP):
                tile = scores[k, r : r + STEP, lanes] + u_ref[a, r : r + STEP, :]
                tile = jnp.exp(tile.reshape(STEP // 8, 8, 128) - peak[None])
                total = total + jnp.sum(tile, axis=0)
                tile = tile.reshape(STEP, 128)
                high = tile.astype(jnp.bfloat16)
                hi_ref[r : r + STEP, lanes] = high
                lo_ref[r : r + STEP, lanes] = (tile - high.astype(f32)).astype(jnp.bfloat16)
            s_ref[b, :, lanes] = total
        rows = texts[a]
        dims = (((0,), (0,)), ((), ()))
        acc[b] += lax.dot_general(
            hi_ref[...], rows, dims, preferred_element_type=f32
        ) + lax.dot_general(lo_ref[...], rows, dims, preferred_element_type=f32)

    slots(cnt, pairs, totals)
    sums = jnp.concatenate(col_lse(m_ref, s_ref, lse_out), axis=0)
    spread_columns(jnp.where(sums > 0, 1.0 / sums, 0.0), u_ref)
    y, c = place[1], place[2]
    for r in range(NY):
        b0 = 2 * lax.rem(y + r, NY)
        for z in range(NZ):
            b = b0 + z // 4
            for out, core in ((keep, c), (send, 1 - c)):
                rows = pl.ds(pl.multiple_of((z % 4) * 64 + core * 32, 32), 32)
                scale = u_ref[b, rows, :]
                for q in range(0, D, 128):
                    out[r, z, :, q : q + 128] = acc[b, rows, q : q + 128] * scale


def scale_kernel(place, parts, mass, mine, other, keep, got, after, *refs):
    outs = refs[:8]
    f0_ref, f1_ref = refs[8:]
    v = mass[...] - lse_stack(parts)
    total = jnp.sum(jnp.exp(parts[...] + v[None]), axis=0)
    spread_columns(jnp.exp(mine[...] + v) / total, f0_ref)
    spread_columns(jnp.exp(other[...] + v) / total, f1_ref)
    y, c = place[1], place[2]
    for r in range(NY):
        b0 = 2 * lax.rem(y + r, NY)
        for z in range(NZ):
            b = b0 + z // 4
            rows = pl.ds(pl.multiple_of((z % 4) * 64 + c * 32, 32), 32)
            f0, f1 = f0_ref[b, rows, :], f1_ref[b, rows, :]
            for q in range(0, D, 128):
                lanes = slice(q, q + 128)
                outs[2 * r + z // 4][z % 4, :, lanes] = (
                    keep[r, z, :, lanes] * f0 + got[r, z, :, lanes] * f1
                )


def final_kernel(cnt, pairs, place, held, parts, mass, u, image, *refs):
    src_out = refs[:8]
    scores, sem, images, isem, v_ref, u_ref, w_ref, src_acc, rsum, rmass = refs[8:]
    arrive = fetch_scores(cnt, held, scores, sem)
    copies = fetch_blocks(image, images, isem)
    v_ref[...] = mass[...] - lse_stack(parts)
    spread_columns(u[...], u_ref)
    src_acc[...] = jnp.zeros(src_acc.shape, f32)
    rsum[...] = jnp.zeros(rsum.shape, f32)
    for copy in copies:
        copy.wait()

    def body(k, a, b):
        arrive(k)
        v = v_ref[pl.ds(b, 1), :]
        for r in range(0, BLK, STEP):
            rows = slice(r, r + STEP)
            for half in range(2):
                lanes = slice(half * 128, half * 128 + 128)
                plan = jnp.exp(scores[k, rows, lanes] + u_ref[a, rows, :] + v[:, lanes])
                rsum[a, rows, :] += plan
                w_ref[rows, lanes] = plan.astype(jnp.bfloat16)
        src_acc[a] += jnp.dot(
            w_ref[...], images[b], preferred_element_type=f32
        )

    slots(cnt, pairs, body)
    rmass[...] = columns_to_rows(
        [
            jnp.broadcast_to(jnp.sum(rsum[a], axis=1, keepdims=True), (BLK, 128))
            for a in range(NB)
        ]
    )
    x = place[0]
    for r in range(NB):
        a = lax.rem(2 * x + r, NB)
        src_out[r][:BLK, :] = src_acc[a]
        src_out[r][BLK:, :BLK] = jnp.broadcast_to(rmass[pl.ds(a, 1), :], (8, BLK))
        src_out[r][BLK:, BLK:] = jnp.zeros((8, D - BLK), f32)


def src_norm_kernel(own, plus, minus, out):
    total = own[...] + plus[...] + minus[...]
    cols = to_columns(total[BLK:, :BLK])
    out[...] = total[:BLK, :] / cols[:, :1]


def call(kernel, outs, args, smem, scratch=(), mib=50, hbm=(), flops=1 << 24):
    n = len(args)
    specs = [SMEM if i < smem else HBM if i in hbm else VMEM for i in range(n)]
    flat, tree = jax.tree.flatten(outs)
    out_specs = tree.unflatten([HBM if n + i in hbm else VMEM for i in range(len(flat))])
    return pl.pallas_call(
        kernel,
        out_shape=outs,
        in_specs=specs,
        out_specs=out_specs,
        scratch_shapes=list(scratch),
        compiler_params=pltpu.CompilerParams(vmem_limit_bytes=mib << 20),
        cost_estimate=pl.CostEstimate(
            flops=flops, bytes_accessed=8 << 20, transcendentals=CAP * BLK * BLK
        ),
    )(*args)


def sds(*shape):
    return jax.ShapeDtypeStruct(shape, f32)


def shift(a, axis, size, by):
    return lax.ppermute(a, axis, [(i, (i + by) % size) for i in range(size)])


def over_x(part):
    return [part] + [shift(part, "x", NX, k) for k in (1, 3, 2)]


def over_src(part):
    other = shift(part, "c", NC, 1)
    both = lse_of([part, other])
    copies = jnp.broadcast_to(both[None], (NY * NZ, NB, BLK))
    return lax.all_to_all(copies, ("y", "z"), 0, 0, tiled=True), other


def ring_scatter(own_a, own_b, plus_a, plus_b, far_a, far_b, minus_a, minus_b, axis, size):
    def move(value, by):
        return shift(value, axis, size, by)

    relay_up = move(far_a, 1)
    relay_down = move(far_b, -1)
    from_below_b = move(plus_b, 1)
    from_above_a = move(minus_a, -1)
    from_below_a = move(plus_a + relay_up, 1)
    from_above_b = move(minus_b + relay_down, -1)
    return (own_a, from_below_a, from_above_a), (own_b, from_below_b, from_above_b)


def program(text, image, log_mass_src, log_mass_tgt, pairs, count):
    mass_src = log_mass_src.reshape(NB, BLK)
    mass_tgt = log_mass_tgt.reshape(NB, BLK)
    pairs = pairs[:, 0] * NB + pairs[:, 1]
    place = jnp.stack([lax.axis_index("x"), lax.axis_index("y"), lax.axis_index("c")])
    row_scratch = [pltpu.VMEM((NB, BLK, 128), f32)] * 2
    col_scratch = [pltpu.VMEM((NB, BLK, 128), f32)] + [pltpu.VMEM((NB, 8, BLK), f32)] * 2
    tiles = [pltpu.VMEM((CAP, BLK, BLK), f32), pltpu.SemaphoreType.DMA((CAP,))]
    blocks = [pltpu.VMEM((NB, BLK, D), jnp.bfloat16)]
    block_sem = [pltpu.SemaphoreType.DMA((NB,))]
    stats = sds(NB, BLK)
    scores, part = call(
        first_kernel,
        (sds(CAP, BLK, BLK), stats),
        (count, pairs, text, image),
        2,
        row_scratch + tiles[:1] + blocks * 2 + tiles[1:] + block_sem * 2,
        52,
        (2, 3, 4),
        1 << 30,
    )
    for _ in range(ITERS - 1):
        part = call(
            col_kernel,
            stats,
            (count, pairs, scores, *over_x(part), mass_src),
            2,
            col_scratch + tiles,
            hbm=(2,),
        )
        stack, _ = over_src(part)
        part = call(
            row_kernel,
            stats,
            (count, pairs, scores, stack, mass_tgt),
            2,
            [pltpu.VMEM((NB, BLK), f32)] + row_scratch + tiles,
            hbm=(2,),
        )
    half = sds(NY, NZ, 32, D)
    mine, u, keep, send = call(
        last_col_kernel,
        (stats, stats, half, half),
        (count, pairs, place, scores, *over_x(part), mass_src, text),
        3,
        col_scratch
        + tiles
        + blocks
        + block_sem
        + [pltpu.VMEM((BLK, BLK), jnp.bfloat16)] * 2
        + [pltpu.VMEM((NB, BLK, D), f32)],
        50,
        (3, 9),
        1 << 31,
    )
    stack, other = over_src(mine)
    got = shift(send, "c", NC, 1)
    outs = call(
        final_kernel,
        tuple([sds(BLK + 8, D)] * 8),
        (count, pairs, place, scores, stack, mass_tgt, u, image),
        3,
        tiles
        + blocks
        + block_sem
        + [
            pltpu.VMEM((NB, BLK), f32),
            pltpu.VMEM((NB, BLK, 128), f32),
            pltpu.VMEM((BLK, BLK), jnp.bfloat16),
            pltpu.VMEM((NB, BLK, D), f32),
            pltpu.VMEM((NB, BLK, 128), f32),
            pltpu.VMEM((NB, BLK), f32),
        ],
        50,
        (3, 7),
        1 << 30,
    )
    halves = call(
        scale_kernel,
        tuple([sds(4, 32, D)] * 8),
        (place, stack, mass_tgt, mine, other, keep, got, outs[4]),
        1,
        [pltpu.VMEM((NB, BLK, 128), f32)] * 2,
        16,
        (7,),
    )
    part_a, part_b = ring_scatter(*outs, "x", NX)
    tgt_a, tgt_b = ring_scatter(*halves, "y", NY)
    summed = jnp.concatenate([sum(tgt_a), sum(tgt_b)], axis=0)
    got = lax.all_to_all(summed, "z", 0, 0, tiled=True)
    tgt_map = jnp.sum(got, axis=0)
    src_map = jnp.concatenate(
        [call(src_norm_kernel, sds(BLK, D), p, 0, (), 16) for p in (part_a, part_b)],
        axis=0,
    )
    return (src_map, tgt_map.reshape(32, D))


def solution(mesh):
    grid = Mesh(mesh.devices.reshape(NY, NZ, NC, NX), ("y", "z", "c", "x"))
    src = ("y", "z", "c")
    return jax.shard_map(
        program,
        mesh=grid,
        in_specs=(P(src, None), P("x", None), P(src), P("x"), P((*src, "x"), None), P((*src, "x"))),
        out_specs=(P((*src, "x"), None), P(("x", *src), None)),
        check_vma=False,
    )
```

```python
import functools

import jax
import jax.numpy as jnp
from jax import lax
from jax.experimental import pallas as pl
from jax.experimental.pallas import tpu as pltpu
from jax.sharding import Mesh, PartitionSpec as P


BLK = 256
ITERS = 3
NB = 8
CAP = 16
D = 512
NX, NY, NZ, NC = 4, 4, 8, 2
FLOOR = -1e30
INV_TEMP = 0.15
STEP = 64


VMEM = pl.BlockSpec(memory_space=pltpu.VMEM)
SMEM = pl.BlockSpec(memory_space=pltpu.SMEM)
HBM = pl.BlockSpec(memory_space=pltpu.HBM)
f32 = jnp.float32


def lse_of(parts):
    peak = functools.reduce(jnp.maximum, parts)
    total = sum(jnp.exp(p - peak) for p in parts)
    return peak + jnp.log(total)


def lse_stack(ref):
    peak = jnp.max(ref[...], axis=0)
    total = jnp.sum(jnp.exp(ref[...] - peak[None]), axis=0)
    return peak + jnp.log(total)


def slots(cnt, pairs, body):
    def step(k, _):
        pair = pairs[k]
        body(k, pair // NB, pair % NB)
        return 0

    lax.fori_loop(0, cnt[0], step, 0)


def every_slot(cnt, act):
    def step(k, _):
        act(k)
        return 0

    lax.fori_loop(0, cnt[0], step, 0)


def fetch_scores(cnt, held, scores, sem):
    every_slot(cnt, lambda k: pltpu.make_async_copy(held.at[k], scores.at[k], sem.at[k]).start())
    return lambda k: pltpu.make_async_copy(held.at[k], scores.at[k], sem.at[k]).wait()


def fetch_blocks(held, out, sem):
    copies = [
        pltpu.make_async_copy(held.at[pl.ds(i * BLK, BLK), :], out.at[i], sem.at[i])
        for i in range(NB)
    ]
    for copy in copies:
        copy.start()
    return copies


def to_columns(rows):
    padded = jnp.concatenate([rows, jnp.zeros((120, BLK), f32)], axis=0)
    return jnp.transpose(padded)


def spread_columns(rows, out):
    cols = to_columns(rows)
    for a in range(NB):
        out[a] = jnp.broadcast_to(cols[:, a : a + 1], (BLK, 128))


def columns_to_rows(columns):
    lane = lax.broadcasted_iota(jnp.int32, (BLK, 128), 1)
    table = jnp.zeros((BLK, 128), f32)
    for a, column in enumerate(columns):
        table = jnp.where(lane == a, column, table)
    return jnp.transpose(table)[:NB]


def row_totals(cnt, pairs, scores, v, m_ref, s_ref, lse_out):
    s_ref[...] = jnp.zeros(s_ref.shape, f32)

    def body(k, a, b):
        shift = v[pl.ds(b, 1), :] if v is not None else None
        for r in range(0, BLK, STEP):
            rows = slice(r, r + STEP)
            tile = scores[k, rows, :]
            if shift is not None:
                tile = tile + shift
            peak = m_ref[a, rows, :]
            s_ref[a, rows, :] += jnp.exp(tile[:, :128] - peak) + jnp.exp(tile[:, 128:] - peak)

    slots(cnt, pairs, body)
    for a in range(NB):
        for h in range(0, BLK, 128):
            rows = slice(h, h + 128)
            peaks = jnp.transpose(m_ref[a, rows, :])
            totals = jnp.transpose(s_ref[a, rows, :])
            peak = jnp.max(peaks, axis=0, keepdims=True)
            total = jnp.sum(totals * jnp.exp(peaks - peak), axis=0, keepdims=True)
            lse_out[a : a + 1, rows] = jnp.where(total > 0, peak + jnp.log(total), FLOOR)


def first_kernel(
    cnt, pairs, text, image, held, lse_out, m_ref, s_ref, scores, texts, images, sem, tsem, isem
):
    copies = fetch_blocks(text, texts, tsem) + fetch_blocks(image, images, isem)
    m_ref[...] = jnp.full(m_ref.shape, FLOOR, f32)
    for copy in copies:
        copy.wait()

    last = cnt[0] - 1

    def two(i, _):
        picks = []
        for k in (2 * i, jnp.minimum(2 * i + 1, last)):
            pair = pairs[k]
            a, b = pair // NB, pair % NB
            tile = lax.dot_general(
                texts[a], images[b], (((1,), (1,)), ((), ())), preferred_element_type=f32
            )
            picks.append((k, a, tile * INV_TEMP))
        for k, a, tile in picks:
            scores[k] = tile
            m_ref[a] = jnp.maximum(m_ref[a], jnp.maximum(tile[:, :128], tile[:, 128:]))
        return 0

    lax.fori_loop(0, (cnt[0] + 1) // 2, two, 0)
    every_slot(cnt, lambda k: pltpu.make_async_copy(scores.at[k], held.at[k], sem.at[k]).start())
    row_totals(cnt, pairs, scores, None, m_ref, s_ref, lse_out)
    every_slot(cnt, lambda k: pltpu.make_async_copy(scores.at[k], held.at[k], sem.at[k]).wait())


def row_sums(cnt, pairs, tile_of, s_ref, out):
    s_ref[...] = jnp.zeros(s_ref.shape, f32)

    def body(k, a, b):
        for r in range(0, BLK, STEP):
            rows = slice(r, r + STEP)
            tile = tile_of(k, a, b, rows)
            s_ref[a, rows, :] += tile[:, :128] + tile[:, 128:]

    slots(cnt, pairs, body)
    for a in range(NB):
        for h in range(0, BLK, 128):
            rows = slice(h, h + 128)
            out[a : a + 1, rows] = jnp.sum(jnp.transpose(s_ref[a, rows, :]), axis=0, keepdims=True)


def plan_kernel(
    cnt, pairs, held, parts, mass, u, plan, out, v_ref, u_ref, s_ref, scores, sem, out_sem
):
    arrive = fetch_scores(cnt, held, scores, sem)
    v_ref[...] = mass[...] - lse_stack(parts)
    spread_columns(u[...], u_ref)

    def tile_of(k, a, b, rows):
        if rows.start == 0:
            arrive(k)
        tile = scores[k, rows, :] + v_ref[pl.ds(b, 1), :]
        shift = u_ref[a, rows, :]
        tile = jnp.exp(tile + jnp.concatenate([shift, shift], axis=1))
        scores[k, rows, :] = tile
        if rows.stop == BLK:
            pltpu.make_async_copy(scores.at[k], plan.at[k], out_sem.at[k]).start()
        return tile

    row_sums(cnt, pairs, tile_of, s_ref, out)
    every_slot(cnt, lambda k: pltpu.make_async_copy(scores.at[k], plan.at[k], out_sem.at[k]).wait())


def row_kernel(cnt, pairs, held, parts, mass, out, b_ref, s_ref, plan, sem):
    arrive = fetch_scores(cnt, held, plan, sem)
    b_ref[...] = jnp.exp(mass[...]) / jnp.sum(parts[...], axis=0)

    def tile_of(k, a, b, rows):
        if rows.start == 0:
            arrive(k)
        return plan[k, rows, :] * b_ref[pl.ds(b, 1), :]

    row_sums(cnt, pairs, tile_of, s_ref, out)


def col_peaks(cnt, pairs, scores, arrive, u, u_ref, m_ref, s_ref):
    spread_columns(u, u_ref)
    m_ref[...] = jnp.full(m_ref.shape, FLOOR, f32)
    s_ref[...] = jnp.zeros(s_ref.shape, f32)

    def peaks(k, a, b):
        arrive(k)
        for half in range(2):
            lanes = slice(half * 128, half * 128 + 128)
            best = m_ref[b, :, lanes]
            for r in range(0, BLK, STEP):
                tile = scores[k, r : r + STEP, lanes] + u_ref[a, r : r + STEP, :]
                best = jnp.maximum(best, jnp.max(tile.reshape(STEP // 8, 8, 128), axis=0))
            m_ref[b, :, lanes] = best

    slots(cnt, pairs, peaks)
    for b in range(NB):
        m_ref[b] = jnp.broadcast_to(jnp.max(m_ref[b], axis=0, keepdims=True), (8, BLK))


def col_lse(m_ref, s_ref, lse_out):
    for b in range(NB):
        total = jnp.sum(s_ref[b], axis=0, keepdims=True)
        lse_out[b : b + 1, :] = jnp.where(total > 0, m_ref[b, :1, :] + jnp.log(total), FLOOR)


def col_kernel(
    cnt, pairs, held, p0, p1, p2, p3, mass, lse_out, u_out, u_ref, m_ref, s_ref, scores, sem
):
    arrive = fetch_scores(cnt, held, scores, sem)
    u = mass[...] - lse_of([p0[...], p1[...], p2[...], p3[...]])
    u_out[...] = u
    col_peaks(cnt, pairs, scores, arrive, u, u_ref, m_ref, s_ref)

    def totals(k, a, b):
        for half in range(2):
            lanes = slice(half * 128, half * 128 + 128)
            peak = m_ref[b, :, lanes]
            total = s_ref[b, :, lanes]
            for r in range(0, BLK, STEP):
                tile = scores[k, r : r + STEP, lanes] + u_ref[a, r : r + STEP, :]
                tile = jnp.exp(tile.reshape(STEP // 8, 8, 128) - peak[None])
                total = total + jnp.sum(tile, axis=0)
            s_ref[b, :, lanes] = total

    slots(cnt, pairs, totals)
    col_lse(m_ref, s_ref, lse_out)


def col_sum_kernel(cnt, pairs, held, p0, p1, p2, p3, mass, out, a_ref, s_ref, plan, sem):
    arrive = fetch_scores(cnt, held, plan, sem)
    spread_columns(jnp.exp(mass[...]) / (p0[...] + p1[...] + p2[...] + p3[...]), a_ref)
    s_ref[...] = jnp.zeros(s_ref.shape, f32)

    def body(k, a, b):
        arrive(k)
        for half in range(2):
            lanes = slice(half * 128, half * 128 + 128)
            total = s_ref[b, :, lanes]
            for r in range(0, BLK, STEP):
                tile = plan[k, r : r + STEP, lanes] * a_ref[a, r : r + STEP, :]
                total = total + jnp.sum(tile.reshape(STEP // 8, 8, 128), axis=0)
            s_ref[b, :, lanes] = total

    slots(cnt, pairs, body)
    for b in range(NB):
        out[b : b + 1, :] = jnp.sum(s_ref[b], axis=0, keepdims=True)


def last_col_kernel(
    cnt, pairs, place, held, p0, p1, p2, p3, mass, text, out, a_out, keep, send,
    a_ref, s_ref, plan, sem, texts, tsem, w_ref, acc,
):
    arrive = fetch_scores(cnt, held, plan, sem)
    copies = fetch_blocks(text, texts, tsem)
    scale = jnp.exp(mass[...]) / (p0[...] + p1[...] + p2[...] + p3[...])
    a_out[...] = scale
    spread_columns(scale, a_ref)
    s_ref[...] = jnp.zeros(s_ref.shape, f32)
    acc[...] = jnp.zeros(acc.shape, f32)
    for copy in copies:
        copy.wait()

    def body(k, a, b):
        arrive(k)
        for half in range(2):
            lanes = slice(half * 128, half * 128 + 128)
            total = s_ref[b, :, lanes]
            for r in range(0, BLK, STEP):
                tile = plan[k, r : r + STEP, lanes] * a_ref[a, r : r + STEP, :]
                total = total + jnp.sum(tile.reshape(STEP // 8, 8, 128), axis=0)
                w_ref[r : r + STEP, lanes] = tile.astype(jnp.bfloat16)
            s_ref[b, :, lanes] = total
        acc[b] += lax.dot_general(
            w_ref[...], texts[a], (((0,), (0,)), ((), ())), preferred_element_type=f32
        )

    slots(cnt, pairs, body)
    for b in range(NB):
        out[b : b + 1, :] = jnp.sum(s_ref[b], axis=0, keepdims=True)
    y, c = place[1], place[2]
    for r in range(NY):
        b0 = 2 * lax.rem(y + r, NY)
        for z in range(NZ):
            b = b0 + z // 4
            for dst, core in ((keep, c), (send, 1 - c)):
                dst[r, z] = acc[b, pl.ds(pl.multiple_of((z % 4) * 64 + core * 32, 32), 32), :]


def add_kernel(keep, got, *outs):
    for r in range(NY):
        for h in range(2):
            outs[2 * r + h][...] = keep[r, 4 * h : 4 * h + 4] + got[r, 4 * h : 4 * h + 4]


def tgt_norm_kernel(place, parts, stack, out, c_ref):
    y, c, z = place[1], place[2], place[3]
    b = 2 * y + z // 4
    lane = lax.broadcasted_iota(jnp.int32, (BLK, 128), 1)
    cols = to_columns(jnp.sum(stack[...], axis=0))
    c_ref[...] = jnp.where(lane == b, cols, 0.0)
    rows = pl.ds(pl.multiple_of(lax.rem(z, 4) * 64 + c * 32, 32), 32)
    mass = jnp.sum(c_ref[rows, :], axis=1, keepdims=True)
    out[...] = jnp.sum(parts[...], axis=0) / mass


def final_kernel(offset, cnt, pairs, place, held, parts, mass, scale, image, *refs):
    src_out = refs[:4]
    scores, sem, images, isem, b_ref, a_ref, w_ref, acc, rsum = refs[4:]
    start = 2 * place[0] + offset

    def mine(act):
        def step(k, _):
            pair = pairs[k]
            a = pair // NB
            q = lax.rem(a + 2 * NB - start, NB)

            @pl.when(q < 4)
            def _():
                act(k, q, a, pair % NB)

            return 0

        lax.fori_loop(0, cnt[0], step, 0)

    mine(lambda k, q, a, b: pltpu.make_async_copy(held.at[k], scores.at[k], sem.at[k]).start())
    copies = fetch_blocks(image, images, isem)
    b_ref[...] = jnp.exp(mass[...]) / jnp.sum(parts[...], axis=0)
    spread_columns(scale[...], a_ref)
    acc[...] = jnp.zeros(acc.shape, f32)
    rsum[...] = jnp.zeros(rsum.shape, f32)
    for copy in copies:
        copy.wait()

    def body(k, q, a, b):
        pltpu.make_async_copy(held.at[k], scores.at[k], sem.at[k]).wait()
        v = b_ref[pl.ds(b, 1), :]
        for r in range(0, BLK, STEP):
            rows = slice(r, r + STEP)
            for half in range(2):
                lanes = slice(half * 128, half * 128 + 128)
                plan = scores[k, rows, lanes] * a_ref[a, rows, :] * v[:, lanes]
                rsum[q, rows, :] += plan
                w_ref[rows, lanes] = plan.astype(jnp.bfloat16)
        acc[q] += jnp.dot(w_ref[...], images[b], preferred_element_type=f32)

    mine(body)
    masses = columns_to_rows([jnp.sum(rsum[q], axis=1, keepdims=True) for q in range(4)])
    for q in range(4):
        src_out[q][:BLK, :] = acc[q]
        src_out[q][BLK:, :BLK] = jnp.broadcast_to(masses[q : q + 1, :], (8, BLK))
        src_out[q][BLK:, BLK:] = jnp.zeros((8, D - BLK), f32)


def src_norm_kernel(*refs):
    out = refs[-1]
    for h in range(2):
        own, plus, minus = refs[3 * h : 3 * h + 3]
        rows = slice(BLK, BLK + 8)
        mass = own[rows, :BLK] + plus[rows, :BLK] + minus[rows, :BLK]
        scale = to_columns(1.0 / mass)[:, :1]
        out[h * BLK : h * BLK + BLK, :] = (
            own[:BLK, :] + plus[:BLK, :] + minus[:BLK, :]
        ) * scale


def call(kernel, outs, args, smem, scratch=(), mib=50, hbm=(), flops=1 << 24):
    n = len(args)
    specs = [SMEM if i < smem else HBM if i in hbm else VMEM for i in range(n)]
    flat, tree = jax.tree.flatten(outs)
    out_specs = tree.unflatten([HBM if n + i in hbm else VMEM for i in range(len(flat))])
    return pl.pallas_call(
        kernel,
        out_shape=outs,
        in_specs=specs,
        out_specs=out_specs,
        scratch_shapes=list(scratch),
        compiler_params=pltpu.CompilerParams(vmem_limit_bytes=mib << 20),
        cost_estimate=pl.CostEstimate(
            flops=flops, bytes_accessed=8 << 20, transcendentals=CAP * BLK * BLK
        ),
    )(*args)


def sds(*shape):
    return jax.ShapeDtypeStruct(shape, f32)


def shift(a, axis, size, by):
    return lax.ppermute(a, axis, [(i, (i + by) % size) for i in range(size)])


def over_x(part):
    return [part] + [shift(part, "x", NX, k) for k in (1, 3, 2)]


def over_src(part, join):
    other = shift(part, "c", NC, 1)
    both = join([part, other])
    copies = jnp.broadcast_to(both[None], (NY * NZ, NB, BLK))
    return lax.all_to_all(copies, ("y", "z"), 0, 0, tiled=True)


def ring_scatter(own_a, own_b, plus_a, plus_b, far_a, far_b, minus_a, minus_b, axis, size):
    def move(value, by):
        return shift(value, axis, size, by)

    relay_up = move(far_a, 1)
    relay_down = move(far_b, -1)
    from_below_b = move(plus_b, 1)
    from_above_a = move(minus_a, -1)
    from_below_a = move(plus_a + relay_up, 1)
    from_above_b = move(minus_b + relay_down, -1)
    return (own_a, from_below_a, from_above_a), (own_b, from_below_b, from_above_b)


def program(text, image, log_mass_src, log_mass_tgt, pairs, count):
    mass_src = log_mass_src.reshape(NB, BLK)
    mass_tgt = log_mass_tgt.reshape(NB, BLK)
    pairs = pairs[:, 0] * NB + pairs[:, 1]
    place = jnp.stack([lax.axis_index(name) for name in ("x", "y", "c", "z")])
    row_scratch = [pltpu.VMEM((NB, BLK, 128), f32)] * 2
    col_scratch = [pltpu.VMEM((NB, BLK, 128), f32)] + [pltpu.VMEM((NB, 8, BLK), f32)] * 2
    tiles = [pltpu.VMEM((CAP, BLK, BLK), f32), pltpu.SemaphoreType.DMA((CAP,))]
    blocks = [pltpu.VMEM((NB, BLK, D), jnp.bfloat16)]
    block_sem = [pltpu.SemaphoreType.DMA((NB,))]
    stats = sds(NB, BLK)
    scores, part = call(
        first_kernel,
        (sds(CAP, BLK, BLK), stats),
        (count, pairs, text, image),
        2,
        row_scratch + tiles[:1] + blocks * 2 + tiles[1:] + block_sem * 2,
        52,
        (2, 3, 4),
        1 << 30,
    )
    part, u = call(
        col_kernel,
        (stats, stats),
        (count, pairs, scores, *over_x(part), mass_src),
        2,
        col_scratch + tiles,
        hbm=(2,),
    )
    stack = over_src(part, lse_of)
    plan, part = call(
        plan_kernel,
        (sds(CAP, BLK, BLK), stats),
        (count, pairs, scores, stack, mass_tgt, u),
        2,
        [pltpu.VMEM((NB, BLK), f32)] + row_scratch + tiles + tiles[1:],
        hbm=(2, 6),
    )
    for _ in range(ITERS - 2):
        part = call(
            col_sum_kernel,
            stats,
            (count, pairs, plan, *over_x(part), mass_src),
            2,
            [col_scratch[0], col_scratch[1]] + tiles,
            hbm=(2,),
        )
        stack = over_src(part, sum)
        part = call(
            row_kernel,
            stats,
            (count, pairs, plan, stack, mass_tgt),
            2,
            [pltpu.VMEM((NB, BLK), f32), row_scratch[0]] + tiles,
            hbm=(2,),
        )
    half = sds(NY, NZ, 32, D)
    part, scale, keep, send = call(
        last_col_kernel,
        (stats, stats, half, half),
        (count, pairs, place, plan, *over_x(part), mass_src, text),
        3,
        [col_scratch[0], col_scratch[1]]
        + tiles
        + blocks
        + block_sem
        + [pltpu.VMEM((BLK, BLK), jnp.bfloat16), pltpu.VMEM((NB, BLK, D), f32)],
        50,
        (3, 9),
        1 << 31,
    )
    got = shift(send, "c", NC, 1)
    stack = over_src(part, sum)
    halves = call(add_kernel, tuple([sds(4, 32, D)] * 8), (keep, got), 0, (), 16)

    def final(offset):
        return call(
            functools.partial(final_kernel, offset),
            tuple([sds(BLK + 8, D)] * 4),
            (count, pairs, place, plan, stack, mass_tgt, scale, image),
            3,
            tiles
            + blocks
            + block_sem
            + [
                pltpu.VMEM((NB, BLK), f32),
                pltpu.VMEM((NB, BLK, 128), f32),
                pltpu.VMEM((BLK, BLK), jnp.bfloat16),
                pltpu.VMEM((4, BLK, D), f32),
                pltpu.VMEM((4, BLK, 128), f32),
            ],
            50,
            (3, 7),
            1 << 29,
        )

    far = final(3)
    near = final(7)
    part_a, part_b = ring_scatter(*near[1:], *far, near[0], "x", NX)
    tgt_a, tgt_b = ring_scatter(*halves, "y", NY)
    summed = jnp.concatenate([sum(tgt_a), sum(tgt_b)], axis=0)
    got = lax.all_to_all(summed, "z", 0, 0, tiled=True)
    tgt_map = call(
        tgt_norm_kernel, sds(32, D), (place, got, stack), 1, [pltpu.VMEM((BLK, 128), f32)], 16
    )
    src_map = call(src_norm_kernel, sds(2 * BLK, D), (*part_a, *part_b), 0, (), 16)
    return (src_map, tgt_map)


def solution(mesh):
    grid = Mesh(mesh.devices.reshape(NY, NZ, NC, NX), ("y", "z", "c", "x"))
    src = ("y", "z", "c")
    return jax.shard_map(
        program,
        mesh=grid,
        in_specs=(P(src, None), P("x", None), P(src), P("x"), P((*src, "x"), None), P((*src, "x"))),
        out_specs=(P((*src, "x"), None), P(("x", *src), None)),
        check_vma=False,
    )
```

```python
import functools

import jax
import jax.numpy as jnp
from jax import lax
from jax.experimental import pallas as pl
from jax.experimental.pallas import tpu as pltpu
from jax.sharding import Mesh, PartitionSpec as P


BLK = 256
ITERS = 3
NB = 8
CAP = 16
D = 512
NX, NY, NZ, NC = 4, 4, 8, 2
FLOOR = -1e30
INV_TEMP = 0.15
STEP = 64


VMEM = pl.BlockSpec(memory_space=pltpu.VMEM)
SMEM = pl.BlockSpec(memory_space=pltpu.SMEM)
HBM = pl.BlockSpec(memory_space=pltpu.HBM)
f32 = jnp.float32


def lse_of(parts):
    peak = functools.reduce(jnp.maximum, parts)
    total = sum(jnp.exp(p - peak) for p in parts)
    return peak + jnp.log(total)


def lse_stack(ref):
    peak = jnp.max(ref[...], axis=0)
    total = jnp.sum(jnp.exp(ref[...] - peak[None]), axis=0)
    return peak + jnp.log(total)


def sum_stack(ref):
    return jnp.sum(ref[...], axis=0)


def both_halves(place, mine, other, join):
    first = place[2] == 0
    a, b = join(mine), join(other)
    return jnp.concatenate([jnp.where(first, a, b), jnp.where(first, b, a)], axis=1)


def hand_out(place, stats, mine, give):
    first = place[2] == 0
    low, high = stats[:, :128], stats[:, 128:]
    mine[...] = jnp.where(first, low, high)
    give[...] = jnp.where(first, high, low)


def slots(cnt, pairs, body):
    def step(k, _):
        pair = pairs[k]
        body(k, pair // NB, pair % NB)
        return 0

    lax.fori_loop(0, cnt[0], step, 0)


def every_slot(cnt, act):
    def step(k, _):
        act(k)
        return 0

    lax.fori_loop(0, cnt[0], step, 0)


def fetch_scores(cnt, held, scores, sem):
    every_slot(cnt, lambda k: pltpu.make_async_copy(held.at[k], scores.at[k], sem.at[k]).start())
    return lambda k: pltpu.make_async_copy(held.at[k], scores.at[k], sem.at[k]).wait()


def fetch_blocks(held, out, sem):
    copies = [
        pltpu.make_async_copy(held.at[pl.ds(i * BLK, BLK), :], out.at[i], sem.at[i])
        for i in range(NB)
    ]
    for copy in copies:
        copy.start()
    return copies


def to_columns(rows):
    padded = jnp.concatenate([rows, jnp.zeros((120, BLK), f32)], axis=0)
    return jnp.transpose(padded)


def spread_columns(rows, out):
    cols = to_columns(rows)
    for a in range(NB):
        out[a] = jnp.broadcast_to(cols[:, a : a + 1], (BLK, 128))


def columns_to_rows(columns):
    lane = lax.broadcasted_iota(jnp.int32, (BLK, 128), 1)
    table = jnp.zeros((BLK, 128), f32)
    for a, column in enumerate(columns):
        table = jnp.where(lane == a, column, table)
    return jnp.transpose(table)[:NB]


def row_totals(cnt, pairs, scores, v, m_ref, s_ref, lse_out):
    s_ref[...] = jnp.zeros(s_ref.shape, f32)

    def body(k, a, b):
        shift = v[pl.ds(b, 1), :] if v is not None else None
        for r in range(0, BLK, STEP):
            rows = slice(r, r + STEP)
            tile = scores[k, rows, :]
            if shift is not None:
                tile = tile + shift
            peak = m_ref[a, rows, :]
            s_ref[a, rows, :] += jnp.exp(tile[:, :128] - peak) + jnp.exp(tile[:, 128:] - peak)

    slots(cnt, pairs, body)
    for a in range(NB):
        for h in range(0, BLK, 128):
            rows = slice(h, h + 128)
            peaks = jnp.transpose(m_ref[a, rows, :])
            totals = jnp.transpose(s_ref[a, rows, :])
            peak = jnp.max(peaks, axis=0, keepdims=True)
            total = jnp.sum(totals * jnp.exp(peaks - peak), axis=0, keepdims=True)
            lse_out[a : a + 1, rows] = jnp.where(total > 0, peak + jnp.log(total), FLOOR)


def first_kernel(
    cnt, pairs, text, image, held, lse_out, m_ref, s_ref, scores, texts, images, sem, tsem, isem
):
    copies = fetch_blocks(text, texts, tsem) + fetch_blocks(image, images, isem)
    m_ref[...] = jnp.full(m_ref.shape, FLOOR, f32)
    for copy in copies:
        copy.wait()

    last = cnt[0] - 1

    def two(i, _):
        picks = []
        for k in (2 * i, jnp.minimum(2 * i + 1, last)):
            pair = pairs[k]
            a, b = pair // NB, pair % NB
            tile = lax.dot_general(
                texts[a], images[b], (((1,), (1,)), ((), ())), preferred_element_type=f32
            )
            picks.append((k, a, tile * INV_TEMP))
        for k, a, tile in picks:
            scores[k] = tile
            m_ref[a] = jnp.maximum(m_ref[a], jnp.maximum(tile[:, :128], tile[:, 128:]))
        return 0

    lax.fori_loop(0, (cnt[0] + 1) // 2, two, 0)
    every_slot(cnt, lambda k: pltpu.make_async_copy(scores.at[k], held.at[k], sem.at[k]).start())
    row_totals(cnt, pairs, scores, None, m_ref, s_ref, lse_out)
    every_slot(cnt, lambda k: pltpu.make_async_copy(scores.at[k], held.at[k], sem.at[k]).wait())


def row_sums(cnt, pairs, tile_of, s_ref, out):
    s_ref[...] = jnp.zeros(s_ref.shape, f32)

    def body(k, a, b):
        for r in range(0, BLK, STEP):
            rows = slice(r, r + STEP)
            tile = tile_of(k, a, b, rows)
            s_ref[a, rows, :] += tile[:, :128] + tile[:, 128:]

    slots(cnt, pairs, body)
    for a in range(NB):
        for h in range(0, BLK, 128):
            rows = slice(h, h + 128)
            out[a : a + 1, rows] = jnp.sum(jnp.transpose(s_ref[a, rows, :]), axis=0, keepdims=True)


def plan_kernel(
    cnt, pairs, place, held, mine, other, mass, u, plan, out,
    v_ref, u_ref, s_ref, scores, sem, out_sem,
):
    arrive = fetch_scores(cnt, held, scores, sem)
    v_ref[...] = mass[...] - both_halves(place, mine, other, lse_stack)
    spread_columns(u[...], u_ref)

    def tile_of(k, a, b, rows):
        if rows.start == 0:
            arrive(k)
        tile = scores[k, rows, :] + v_ref[pl.ds(b, 1), :]
        shift = u_ref[a, rows, :]
        tile = jnp.exp(tile + jnp.concatenate([shift, shift], axis=1))
        scores[k, rows, :] = tile
        if rows.stop == BLK:
            pltpu.make_async_copy(scores.at[k], plan.at[k], out_sem.at[k]).start()
        return tile

    row_sums(cnt, pairs, tile_of, s_ref, out)
    every_slot(cnt, lambda k: pltpu.make_async_copy(scores.at[k], plan.at[k], out_sem.at[k]).wait())


def row_kernel(cnt, pairs, place, held, mine, other, mass, out, b_ref, s_ref, plan, sem):
    arrive = fetch_scores(cnt, held, plan, sem)
    b_ref[...] = jnp.exp(mass[...]) / both_halves(place, mine, other, sum_stack)

    def tile_of(k, a, b, rows):
        if rows.start == 0:
            arrive(k)
        return plan[k, rows, :] * b_ref[pl.ds(b, 1), :]

    row_sums(cnt, pairs, tile_of, s_ref, out)


def col_peaks(cnt, pairs, scores, arrive, u, u_ref, m_ref, s_ref):
    spread_columns(u, u_ref)
    m_ref[...] = jnp.full(m_ref.shape, FLOOR, f32)
    s_ref[...] = jnp.zeros(s_ref.shape, f32)

    def peaks(k, a, b):
        arrive(k)
        for half in range(2):
            lanes = slice(half * 128, half * 128 + 128)
            best = m_ref[b, :, lanes]
            for r in range(0, BLK, STEP):
                tile = scores[k, r : r + STEP, lanes] + u_ref[a, r : r + STEP, :]
                best = jnp.maximum(best, jnp.max(tile.reshape(STEP // 8, 8, 128), axis=0))
            m_ref[b, :, lanes] = best

    slots(cnt, pairs, peaks)
    for b in range(NB):
        m_ref[b] = jnp.broadcast_to(jnp.max(m_ref[b], axis=0, keepdims=True), (8, BLK))


def col_lse(place, m_ref, s_ref, mine, give):
    rows = []
    for b in range(NB):
        total = jnp.sum(s_ref[b], axis=0, keepdims=True)
        rows.append(jnp.where(total > 0, m_ref[b, :1, :] + jnp.log(total), FLOOR))
    hand_out(place, jnp.concatenate(rows, axis=0), mine, give)


def col_kernel(
    cnt, pairs, place, held, p0, p1, p2, p3, mass, mine, give, u_out,
    u_ref, m_ref, s_ref, scores, sem,
):
    arrive = fetch_scores(cnt, held, scores, sem)
    u = mass[...] - lse_of([p0[...], p1[...], p2[...], p3[...]])
    u_out[...] = u
    col_peaks(cnt, pairs, scores, arrive, u, u_ref, m_ref, s_ref)

    def totals(k, a, b):
        for half in range(2):
            lanes = slice(half * 128, half * 128 + 128)
            peak = m_ref[b, :, lanes]
            total = s_ref[b, :, lanes]
            for r in range(0, BLK, STEP):
                tile = scores[k, r : r + STEP, lanes] + u_ref[a, r : r + STEP, :]
                tile = jnp.exp(tile.reshape(STEP // 8, 8, 128) - peak[None])
                total = total + jnp.sum(tile, axis=0)
            s_ref[b, :, lanes] = total

    slots(cnt, pairs, totals)
    col_lse(place, m_ref, s_ref, mine, give)


def hand_out_sums(place, s_ref, mine, give):
    sums = [jnp.sum(s_ref[b], axis=0, keepdims=True) for b in range(NB)]
    hand_out(place, jnp.concatenate(sums, axis=0), mine, give)


def col_sum_kernel(
    cnt, pairs, place, held, p0, p1, p2, p3, mass, mine, give, a_ref, s_ref, plan, sem
):
    arrive = fetch_scores(cnt, held, plan, sem)
    spread_columns(jnp.exp(mass[...]) / (p0[...] + p1[...] + p2[...] + p3[...]), a_ref)
    s_ref[...] = jnp.zeros(s_ref.shape, f32)

    def body(k, a, b):
        arrive(k)
        for half in range(2):
            lanes = slice(half * 128, half * 128 + 128)
            total = s_ref[b, :, lanes]
            for r in range(0, BLK, STEP):
                tile = plan[k, r : r + STEP, lanes] * a_ref[a, r : r + STEP, :]
                total = total + jnp.sum(tile.reshape(STEP // 8, 8, 128), axis=0)
            s_ref[b, :, lanes] = total

    slots(cnt, pairs, body)
    hand_out_sums(place, s_ref, mine, give)


def last_col_kernel(
    cnt, pairs, place, held, p0, p1, p2, p3, mass, text, mine, give, a_out, keep, send,
    a_ref, s_ref, plan, sem, texts, tsem, w_ref, acc,
):
    arrive = fetch_scores(cnt, held, plan, sem)
    copies = fetch_blocks(text, texts, tsem)
    scale = jnp.exp(mass[...]) / (p0[...] + p1[...] + p2[...] + p3[...])
    a_out[...] = scale
    spread_columns(scale, a_ref)
    s_ref[...] = jnp.zeros(s_ref.shape, f32)
    acc[...] = jnp.zeros(acc.shape, f32)
    for copy in copies:
        copy.wait()

    def body(k, a, b):
        arrive(k)
        for half in range(2):
            lanes = slice(half * 128, half * 128 + 128)
            total = s_ref[b, :, lanes]
            for r in range(0, BLK, STEP):
                tile = plan[k, r : r + STEP, lanes] * a_ref[a, r : r + STEP, :]
                total = total + jnp.sum(tile.reshape(STEP // 8, 8, 128), axis=0)
                w_ref[r : r + STEP, lanes] = tile.astype(jnp.bfloat16)
            s_ref[b, :, lanes] = total
        acc[b] += lax.dot_general(
            w_ref[...], texts[a], (((0,), (0,)), ((), ())), preferred_element_type=f32
        )

    slots(cnt, pairs, body)
    hand_out_sums(place, s_ref, mine, give)
    y, c = place[1], place[2]
    for r in range(NY):
        b0 = 2 * lax.rem(y + r, NY)
        for z in range(NZ):
            b = b0 + z // 4
            for dst, core in ((keep, c), (send, 1 - c)):
                dst[r, z] = acc[b, pl.ds(pl.multiple_of((z % 4) * 64 + core * 32, 32), 32), :]


def add_kernel(keep, got, *outs):
    for r in range(NY):
        for h in range(2):
            outs[2 * r + h][...] = keep[r, 4 * h : 4 * h + 4] + got[r, 4 * h : 4 * h + 4]


def tgt_norm_kernel(place, parts, mine, other, out, c_ref):
    y, c, z = place[1], place[2], place[3]
    b = 2 * y + z // 4
    lane = lax.broadcasted_iota(jnp.int32, (BLK, 128), 1)
    cols = to_columns(both_halves(place, mine, other, sum_stack))
    c_ref[...] = jnp.where(lane == b, cols, 0.0)
    rows = pl.ds(pl.multiple_of(lax.rem(z, 4) * 64 + c * 32, 32), 32)
    mass = jnp.sum(c_ref[rows, :], axis=1, keepdims=True)
    out[...] = jnp.sum(parts[...], axis=0) / mass


def final_kernel(
    offset, n, cnt, pairs, place, held, mine, other, mass, scale, image, *refs
):
    src_out = refs[:n]
    plan, sem, images, isem, b_ref, r_ref, a_ref, w_ref, acc, rsum = refs[n:]
    start = 2 * place[0] + offset

    def chosen(act):
        def step(k, _):
            pair = pairs[k]
            q = lax.rem(pair // NB + 2 * NB - start, NB)

            @pl.when(q < n)
            def _():
                act(k, q, pair % NB)

            return 0

        lax.fori_loop(0, cnt[0], step, 0)

    def copies(k, b):
        return (
            pltpu.make_async_copy(held.at[k], plan.at[k], sem.at[k]),
            pltpu.make_async_copy(
                image.at[pl.ds(pl.multiple_of(b * BLK, BLK), BLK), :], images.at[k], isem.at[k]
            ),
        )

    @chosen
    def _(k, q, b):
        for copy in copies(k, b):
            copy.start()

    b_ref[...] = jnp.exp(mass[...]) / both_halves(place, mine, other, sum_stack)
    r_ref[...] = jnp.zeros(r_ref.shape, f32)
    for q in range(n):
        r_ref[q : q + 1, :] = scale[pl.ds(lax.rem(start + q, NB), 1), :]
    cols = to_columns(r_ref[...])
    for q in range(n):
        a_ref[q] = jnp.broadcast_to(cols[:, q : q + 1], (BLK, 128))
    acc[...] = jnp.zeros(acc.shape, f32)
    rsum[...] = jnp.zeros(rsum.shape, f32)

    @chosen
    def _(k, q, b):
        for copy in copies(k, b):
            copy.wait()
        v = b_ref[pl.ds(b, 1), :]
        for r in range(0, BLK, STEP):
            rows = slice(r, r + STEP)
            for half in range(2):
                lanes = slice(half * 128, half * 128 + 128)
                tile = plan[k, rows, lanes] * a_ref[q, rows, :] * v[:, lanes]
                rsum[q, rows, :] += tile
                w_ref[rows, lanes] = tile.astype(jnp.bfloat16)
        acc[q] += jnp.dot(w_ref[...], images[k], preferred_element_type=f32)

    masses = columns_to_rows([jnp.sum(rsum[q], axis=1, keepdims=True) for q in range(n)])
    for q in range(n):
        src_out[q][:BLK, :] = acc[q]
        src_out[q][BLK:, :BLK] = jnp.broadcast_to(masses[q : q + 1, :], (8, BLK))
        src_out[q][BLK:, BLK:] = jnp.zeros((8, D - BLK), f32)


def src_norm_kernel(*refs):
    out = refs[-1]
    for h in range(2):
        own, plus, minus = refs[3 * h : 3 * h + 3]
        rows = slice(BLK, BLK + 8)
        mass = own[rows, :BLK] + plus[rows, :BLK] + minus[rows, :BLK]
        scale = to_columns(1.0 / mass)[:, :1]
        out[h * BLK : h * BLK + BLK, :] = (
            own[:BLK, :] + plus[:BLK, :] + minus[:BLK, :]
        ) * scale


def call(kernel, outs, args, smem, scratch=(), mib=50, hbm=(), flops=1 << 24):
    n = len(args)
    specs = [SMEM if i < smem else HBM if i in hbm else VMEM for i in range(n)]
    flat, tree = jax.tree.flatten(outs)
    out_specs = tree.unflatten([HBM if n + i in hbm else VMEM for i in range(len(flat))])
    return pl.pallas_call(
        kernel,
        out_shape=outs,
        in_specs=specs,
        out_specs=out_specs,
        scratch_shapes=list(scratch),
        compiler_params=pltpu.CompilerParams(vmem_limit_bytes=mib << 20),
        cost_estimate=pl.CostEstimate(
            flops=flops, bytes_accessed=8 << 20, transcendentals=CAP * BLK * BLK
        ),
    )(*args)


def sds(*shape):
    return jax.ShapeDtypeStruct(shape, f32)


def shift(a, axis, size, by):
    return lax.ppermute(a, axis, [(i, (i + by) % size) for i in range(size)])


def over_x(part):
    return [part] + [shift(part, "x", NX, k) for k in (1, 3, 2)]


def over_src(mine, give, join):
    got = shift(give, "c", NC, 1)
    both = join([mine, got])
    copies = jnp.broadcast_to(both[None], (NY * NZ, NB, 128))
    stack = lax.all_to_all(copies, ("y", "z"), 0, 0, tiled=True)
    return stack, shift(stack, "c", NC, 1)


def ring_scatter(own_a, own_b, plus_a, plus_b, far_a, far_b, minus_a, minus_b, axis, size):
    def move(value, by):
        return shift(value, axis, size, by)

    relay_up = move(far_a, 1)
    relay_down = move(far_b, -1)
    from_below_b = move(plus_b, 1)
    from_above_a = move(minus_a, -1)
    from_below_a = move(plus_a + relay_up, 1)
    from_above_b = move(minus_b + relay_down, -1)
    return (own_a, from_below_a, from_above_a), (own_b, from_below_b, from_above_b)


def program(text, image, log_mass_src, log_mass_tgt, pairs, count):
    mass_src = log_mass_src.reshape(NB, BLK)
    mass_tgt = log_mass_tgt.reshape(NB, BLK)
    pairs = pairs[:, 0] * NB + pairs[:, 1]
    place = jnp.stack([lax.axis_index(name) for name in ("x", "y", "c", "z")])
    row_scratch = [pltpu.VMEM((NB, BLK, 128), f32)] * 2
    col_scratch = [pltpu.VMEM((NB, BLK, 128), f32)] + [pltpu.VMEM((NB, 8, BLK), f32)] * 2
    tiles = [pltpu.VMEM((CAP, BLK, BLK), f32), pltpu.SemaphoreType.DMA((CAP,))]
    blocks = [pltpu.VMEM((NB, BLK, D), jnp.bfloat16)]
    block_sem = [pltpu.SemaphoreType.DMA((NB,))]
    stats = sds(NB, BLK)
    scores, part = call(
        first_kernel,
        (sds(CAP, BLK, BLK), stats),
        (count, pairs, text, image),
        2,
        row_scratch + tiles[:1] + blocks * 2 + tiles[1:] + block_sem * 2,
        52,
        (2, 3, 4),
        1 << 30,
    )
    lanes = sds(NB, 128)
    mine, give, u = call(
        col_kernel,
        (lanes, lanes, stats),
        (count, pairs, place, scores, *over_x(part), mass_src),
        3,
        col_scratch + tiles,
        hbm=(3,),
    )
    stack = over_src(mine, give, lse_of)
    plan, part = call(
        plan_kernel,
        (sds(CAP, BLK, BLK), stats),
        (count, pairs, place, scores, *stack, mass_tgt, u),
        3,
        [pltpu.VMEM((NB, BLK), f32)] + row_scratch + tiles + tiles[1:],
        hbm=(3, 8),
    )
    for _ in range(ITERS - 2):
        mine, give = call(
            col_sum_kernel,
            (lanes, lanes),
            (count, pairs, place, plan, *over_x(part), mass_src),
            3,
            [col_scratch[0], col_scratch[1]] + tiles,
            hbm=(3,),
        )
        stack = over_src(mine, give, sum)
        part = call(
            row_kernel,
            stats,
            (count, pairs, place, plan, *stack, mass_tgt),
            3,
            [pltpu.VMEM((NB, BLK), f32), row_scratch[0]] + tiles,
            hbm=(3,),
        )
    half = sds(NY, NZ, 32, D)
    mine, give, scale, keep, send = call(
        last_col_kernel,
        (lanes, lanes, stats, half, half),
        (count, pairs, place, plan, *over_x(part), mass_src, text),
        3,
        [col_scratch[0], col_scratch[1]]
        + tiles
        + blocks
        + block_sem
        + [pltpu.VMEM((BLK, BLK), jnp.bfloat16), pltpu.VMEM((NB, BLK, D), f32)],
        50,
        (3, 9),
        1 << 31,
    )
    got = shift(send, "c", NC, 1)
    stack = over_src(mine, give, sum)
    halves = call(add_kernel, tuple([sds(4, 32, D)] * 8), (keep, got), 0, (), 16)

    def final(offset, n):
        return call(
            functools.partial(final_kernel, offset, n),
            tuple([sds(BLK + 8, D)] * n),
            (count, pairs, place, plan, *stack, mass_tgt, scale, image),
            3,
            tiles
            + [
                pltpu.VMEM((CAP, BLK, D), jnp.bfloat16),
                tiles[1],
                pltpu.VMEM((NB, BLK), f32),
                pltpu.VMEM((NB, BLK), f32),
                pltpu.VMEM((n, BLK, 128), f32),
                pltpu.VMEM((BLK, BLK), jnp.bfloat16),
                pltpu.VMEM((n, BLK, D), f32),
                pltpu.VMEM((n, BLK, 128), f32),
            ],
            51,
            (3, 8),
            1 << 29,
        )

    far = final(4, 2)
    near = final(6, 6)
    part_a, part_b = ring_scatter(*near[2:], *far, *near[:2], "x", NX)
    tgt_a, tgt_b = ring_scatter(*halves, "y", NY)
    summed = jnp.concatenate([sum(tgt_a), sum(tgt_b)], axis=0)
    got = lax.all_to_all(summed, "z", 0, 0, tiled=True)
    tgt_map = call(
        tgt_norm_kernel, sds(32, D), (place, got, *stack), 1, [pltpu.VMEM((BLK, 128), f32)], 16
    )
    src_map = call(src_norm_kernel, sds(2 * BLK, D), (*part_a, *part_b), 0, (), 16)
    return (src_map, tgt_map)


def solution(mesh):
    grid = Mesh(mesh.devices.reshape(NY, NZ, NC, NX), ("y", "z", "c", "x"))
    src = ("y", "z", "c")
    return jax.shard_map(
        program,
        mesh=grid,
        in_specs=(P(src, None), P("x", None), P(src), P("x"), P((*src, "x"), None), P((*src, "x"))),
        out_specs=(P((*src, "x"), None), P(("x", *src), None)),
        check_vma=False,
    )
```

```python
import functools

import jax
import jax.numpy as jnp
from jax import lax
from jax.experimental import pallas as pl
from jax.experimental.pallas import tpu as pltpu
from jax.sharding import Mesh, PartitionSpec as P


BLK = 256
ITERS = 3
NB = 8
CAP = 16
D = 512
NX, NY, NZ, NC = 4, 4, 8, 2
FLOOR = -1e30
INV_TEMP = 0.15
STEP = 64


VMEM = pl.BlockSpec(memory_space=pltpu.VMEM)
SMEM = pl.BlockSpec(memory_space=pltpu.SMEM)
HBM = pl.BlockSpec(memory_space=pltpu.HBM)
f32 = jnp.float32


def lse_of(parts):
    peak = functools.reduce(jnp.maximum, parts)
    total = sum(jnp.exp(p - peak) for p in parts)
    return peak + jnp.log(total)


def lse_stack(ref):
    peak = jnp.max(ref[...], axis=0)
    total = jnp.sum(jnp.exp(ref[...] - peak[None]), axis=0)
    return peak + jnp.log(total)


def sum_stack(ref):
    return jnp.sum(ref[...], axis=0)


def both_halves(place, mine, other, join):
    first = place[2] == 0
    a, b = join(mine), join(other)
    return jnp.concatenate([jnp.where(first, a, b), jnp.where(first, b, a)], axis=1)


def hand_out(place, stats, mine, give):
    first = place[2] == 0
    low, high = stats[:, :128], stats[:, 128:]
    mine[...] = jnp.where(first, low, high)
    give[...] = jnp.where(first, high, low)


def slots(cnt, pairs, body):
    def step(k, _):
        pair = pairs[k]
        body(k, pair // NB, pair % NB)
        return 0

    lax.fori_loop(0, cnt[0], step, 0)


def every_slot(cnt, act):
    def step(k, _):
        act(k)
        return 0

    lax.fori_loop(0, cnt[0], step, 0)


def fetch_scores(cnt, held, scores, sem):
    every_slot(cnt, lambda k: pltpu.make_async_copy(held.at[k], scores.at[k], sem.at[k]).start())
    return lambda k: pltpu.make_async_copy(held.at[k], scores.at[k], sem.at[k]).wait()


def fetch_blocks(held, out, sem):
    copies = [
        pltpu.make_async_copy(held.at[pl.ds(i * BLK, BLK), :], out.at[i], sem.at[i])
        for i in range(NB)
    ]
    for copy in copies:
        copy.start()
    return copies


def to_columns(rows):
    padded = jnp.concatenate([rows, jnp.zeros((120, BLK), f32)], axis=0)
    return jnp.transpose(padded)


def spread_columns(rows, out):
    cols = to_columns(rows)
    for a in range(NB):
        out[a] = jnp.broadcast_to(cols[:, a : a + 1], (BLK, 128))


def columns_to_rows(columns):
    lane = lax.broadcasted_iota(jnp.int32, (BLK, 128), 1)
    table = jnp.zeros((BLK, 128), f32)
    for a, column in enumerate(columns):
        table = jnp.where(lane == a, column, table)
    return jnp.transpose(table)[:NB]


def row_totals(cnt, pairs, scores, v, m_ref, s_ref, lse_out):
    s_ref[...] = jnp.zeros(s_ref.shape, f32)

    def body(k, a, b):
        shift = v[pl.ds(b, 1), :] if v is not None else None
        for r in range(0, BLK, STEP):
            rows = slice(r, r + STEP)
            tile = scores[k, rows, :]
            if shift is not None:
                tile = tile + shift
            peak = m_ref[a, rows, :]
            s_ref[a, rows, :] += jnp.exp(tile[:, :128] - peak) + jnp.exp(tile[:, 128:] - peak)

    slots(cnt, pairs, body)
    for a in range(NB):
        for h in range(0, BLK, 128):
            rows = slice(h, h + 128)
            peaks = jnp.transpose(m_ref[a, rows, :])
            totals = jnp.transpose(s_ref[a, rows, :])
            peak = jnp.max(peaks, axis=0, keepdims=True)
            total = jnp.sum(totals * jnp.exp(peaks - peak), axis=0, keepdims=True)
            lse_out[a : a + 1, rows] = jnp.where(total > 0, peak + jnp.log(total), FLOOR)


def first_kernel(
    cnt, pairs, text, image, held, lse_out, m_ref, s_ref, scores, texts, images, sem, tsem, isem
):
    copies = fetch_blocks(text, texts, tsem) + fetch_blocks(image, images, isem)
    m_ref[...] = jnp.full(m_ref.shape, FLOOR, f32)
    for copy in copies:
        copy.wait()

    last = cnt[0] - 1

    def send_out(k):
        pltpu.make_async_copy(scores.at[k], held.at[k], sem.at[k]).start()

    def two(i, _):
        picks = []
        for k in (2 * i, jnp.minimum(2 * i + 1, last)):
            pair = pairs[k]
            a, b = pair // NB, pair % NB
            tile = lax.dot_general(
                texts[a], images[b], (((1,), (1,)), ((), ())), preferred_element_type=f32
            )
            picks.append((k, a, tile * INV_TEMP))
        for k, a, tile in picks:
            scores[k] = tile
            m_ref[a] = jnp.maximum(m_ref[a], jnp.maximum(tile[:, :128], tile[:, 128:]))
        send_out(2 * i)

        @pl.when(2 * i < last)
        def _():
            send_out(2 * i + 1)

        return 0

    lax.fori_loop(0, (cnt[0] + 1) // 2, two, 0)
    row_totals(cnt, pairs, scores, None, m_ref, s_ref, lse_out)
    every_slot(cnt, lambda k: pltpu.make_async_copy(scores.at[k], held.at[k], sem.at[k]).wait())


def row_sums(cnt, pairs, tile_of, s_ref, out):
    s_ref[...] = jnp.zeros(s_ref.shape, f32)

    def body(k, a, b):
        for r in range(0, BLK, STEP):
            rows = slice(r, r + STEP)
            tile = tile_of(k, a, b, rows)
            s_ref[a, rows, :] += tile[:, :128] + tile[:, 128:]

    slots(cnt, pairs, body)
    for a in range(NB):
        for h in range(0, BLK, 128):
            rows = slice(h, h + 128)
            out[a : a + 1, rows] = jnp.sum(jnp.transpose(s_ref[a, rows, :]), axis=0, keepdims=True)


def plan_kernel(
    cnt, pairs, place, held, mine, other, mass, u, plan, out,
    v_ref, u_ref, s_ref, scores, sem, out_sem,
):
    arrive = fetch_scores(cnt, held, scores, sem)
    v_ref[...] = mass[...] - both_halves(place, mine, other, lse_stack)
    spread_columns(u[...], u_ref)

    def tile_of(k, a, b, rows):
        if rows.start == 0:
            arrive(k)
        tile = scores[k, rows, :] + v_ref[pl.ds(b, 1), :]
        shift = u_ref[a, rows, :]
        tile = jnp.exp(tile + jnp.concatenate([shift, shift], axis=1))
        scores[k, rows, :] = tile
        if rows.stop == BLK:
            pltpu.make_async_copy(scores.at[k], plan.at[k], out_sem.at[k]).start()
        return tile

    row_sums(cnt, pairs, tile_of, s_ref, out)
    every_slot(cnt, lambda k: pltpu.make_async_copy(scores.at[k], plan.at[k], out_sem.at[k]).wait())


def row_kernel(cnt, pairs, place, held, mine, other, mass, out, b_ref, s_ref, plan, sem):
    arrive = fetch_scores(cnt, held, plan, sem)
    b_ref[...] = jnp.exp(mass[...]) / both_halves(place, mine, other, sum_stack)

    def tile_of(k, a, b, rows):
        if rows.start == 0:
            arrive(k)
        return plan[k, rows, :] * b_ref[pl.ds(b, 1), :]

    row_sums(cnt, pairs, tile_of, s_ref, out)


def col_peaks(cnt, pairs, scores, arrive, u, u_ref, m_ref, s_ref):
    spread_columns(u, u_ref)
    m_ref[...] = jnp.full(m_ref.shape, FLOOR, f32)
    s_ref[...] = jnp.zeros(s_ref.shape, f32)

    def peaks(k, a, b):
        arrive(k)
        for half in range(2):
            lanes = slice(half * 128, half * 128 + 128)
            best = m_ref[b, :, lanes]
            for r in range(0, BLK, STEP):
                tile = scores[k, r : r + STEP, lanes] + u_ref[a, r : r + STEP, :]
                best = jnp.maximum(best, jnp.max(tile.reshape(STEP // 8, 8, 128), axis=0))
            m_ref[b, :, lanes] = best

    slots(cnt, pairs, peaks)
    for b in range(NB):
        m_ref[b] = jnp.broadcast_to(jnp.max(m_ref[b], axis=0, keepdims=True), (8, BLK))


def col_lse(place, m_ref, s_ref, mine, give):
    rows = []
    for b in range(NB):
        total = jnp.sum(s_ref[b], axis=0, keepdims=True)
        rows.append(jnp.where(total > 0, m_ref[b, :1, :] + jnp.log(total), FLOOR))
    hand_out(place, jnp.concatenate(rows, axis=0), mine, give)


def col_kernel(
    cnt, pairs, place, held, p0, p1, p2, p3, mass, mine, give, u_out,
    u_ref, m_ref, s_ref, scores, sem,
):
    arrive = fetch_scores(cnt, held, scores, sem)
    u = mass[...] - lse_of([p0[...], p1[...], p2[...], p3[...]])
    u_out[...] = u
    col_peaks(cnt, pairs, scores, arrive, u, u_ref, m_ref, s_ref)

    def totals(k, a, b):
        for half in range(2):
            lanes = slice(half * 128, half * 128 + 128)
            peak = m_ref[b, :, lanes]
            total = s_ref[b, :, lanes]
            for r in range(0, BLK, STEP):
                tile = scores[k, r : r + STEP, lanes] + u_ref[a, r : r + STEP, :]
                tile = jnp.exp(tile.reshape(STEP // 8, 8, 128) - peak[None])
                total = total + jnp.sum(tile, axis=0)
            s_ref[b, :, lanes] = total

    slots(cnt, pairs, totals)
    col_lse(place, m_ref, s_ref, mine, give)


def hand_out_sums(place, s_ref, mine, give):
    sums = [jnp.sum(s_ref[b], axis=0, keepdims=True) for b in range(NB)]
    hand_out(place, jnp.concatenate(sums, axis=0), mine, give)


def col_sum_kernel(
    cnt, pairs, place, held, p0, p1, p2, p3, mass, mine, give, a_ref, s_ref, plan, sem
):
    arrive = fetch_scores(cnt, held, plan, sem)
    spread_columns(jnp.exp(mass[...]) / (p0[...] + p1[...] + p2[...] + p3[...]), a_ref)
    s_ref[...] = jnp.zeros(s_ref.shape, f32)

    def body(k, a, b):
        arrive(k)
        for half in range(2):
            lanes = slice(half * 128, half * 128 + 128)
            total = s_ref[b, :, lanes]
            for r in range(0, BLK, STEP):
                tile = plan[k, r : r + STEP, lanes] * a_ref[a, r : r + STEP, :]
                total = total + jnp.sum(tile.reshape(STEP // 8, 8, 128), axis=0)
            s_ref[b, :, lanes] = total

    slots(cnt, pairs, body)
    hand_out_sums(place, s_ref, mine, give)


def last_col_kernel(
    cnt, pairs, place, held, p0, p1, p2, p3, mass, text, mine, give, a_out, keep, send,
    a_ref, s_ref, plan, sem, texts, tsem, w_ref, acc,
):
    arrive = fetch_scores(cnt, held, plan, sem)
    copies = fetch_blocks(text, texts, tsem)
    scale = jnp.exp(mass[...]) / (p0[...] + p1[...] + p2[...] + p3[...])
    a_out[...] = scale
    spread_columns(scale, a_ref)
    s_ref[...] = jnp.zeros(s_ref.shape, f32)
    acc[...] = jnp.zeros(acc.shape, f32)
    for copy in copies:
        copy.wait()

    def body(k, a, b):
        arrive(k)
        for half in range(2):
            lanes = slice(half * 128, half * 128 + 128)
            total = s_ref[b, :, lanes]
            for r in range(0, BLK, STEP):
                tile = plan[k, r : r + STEP, lanes] * a_ref[a, r : r + STEP, :]
                total = total + jnp.sum(tile.reshape(STEP // 8, 8, 128), axis=0)
                w_ref[r : r + STEP, lanes] = tile.astype(jnp.bfloat16)
            s_ref[b, :, lanes] = total
        acc[b] += lax.dot_general(
            w_ref[...], texts[a], (((0,), (0,)), ((), ())), preferred_element_type=f32
        )

    slots(cnt, pairs, body)
    hand_out_sums(place, s_ref, mine, give)
    y, c = place[1], place[2]
    for r in range(NY):
        b0 = 2 * lax.rem(y + r, NY)
        for z in range(NZ):
            b = b0 + z // 4
            for dst, core in ((keep, c), (send, 1 - c)):
                dst[r, z] = acc[b, pl.ds(pl.multiple_of((z % 4) * 64 + core * 32, 32), 32), :]


def add_kernel(keep, got, *outs):
    for r in range(NY):
        for h in range(2):
            outs[2 * r + h][...] = keep[r, 4 * h : 4 * h + 4] + got[r, 4 * h : 4 * h + 4]


def tgt_norm_kernel(place, parts, mine, other, out, c_ref):
    y, c, z = place[1], place[2], place[3]
    b = 2 * y + z // 4
    lane = lax.broadcasted_iota(jnp.int32, (BLK, 128), 1)
    cols = to_columns(both_halves(place, mine, other, sum_stack))
    c_ref[...] = jnp.where(lane == b, cols, 0.0)
    rows = pl.ds(pl.multiple_of(lax.rem(z, 4) * 64 + c * 32, 32), 32)
    mass = jnp.sum(c_ref[rows, :], axis=1, keepdims=True)
    out[...] = jnp.sum(parts[...], axis=0) / mass


def final_kernel(
    offset, n, cnt, pairs, place, held, mine, other, mass, scale, image, *refs
):
    src_out = refs[:n]
    plan, sem, images, isem, b_ref, r_ref, a_ref, w_ref, acc, rsum = refs[n:]
    start = 2 * place[0] + offset

    def chosen(act):
        def step(k, _):
            pair = pairs[k]
            q = lax.rem(pair // NB + 2 * NB - start, NB)

            @pl.when(q < n)
            def _():
                act(k, q, pair % NB)

            return 0

        lax.fori_loop(0, cnt[0], step, 0)

    def copies(k, b):
        return (
            pltpu.make_async_copy(held.at[k], plan.at[k], sem.at[k]),
            pltpu.make_async_copy(
                image.at[pl.ds(pl.multiple_of(b * BLK, BLK), BLK), :], images.at[k], isem.at[k]
            ),
        )

    @chosen
    def _(k, q, b):
        for copy in copies(k, b):
            copy.start()

    b_ref[...] = jnp.exp(mass[...]) / both_halves(place, mine, other, sum_stack)
    r_ref[...] = jnp.zeros(r_ref.shape, f32)
    for q in range(n):
        r_ref[q : q + 1, :] = scale[pl.ds(lax.rem(start + q, NB), 1), :]
    cols = to_columns(r_ref[...])
    for q in range(n):
        a_ref[q] = jnp.broadcast_to(cols[:, q : q + 1], (BLK, 128))
    acc[...] = jnp.zeros(acc.shape, f32)
    rsum[...] = jnp.zeros(rsum.shape, f32)

    @chosen
    def _(k, q, b):
        for copy in copies(k, b):
            copy.wait()
        v = b_ref[pl.ds(b, 1), :]
        for r in range(0, BLK, STEP):
            rows = slice(r, r + STEP)
            for half in range(2):
                lanes = slice(half * 128, half * 128 + 128)
                tile = plan[k, rows, lanes] * a_ref[q, rows, :] * v[:, lanes]
                rsum[q, rows, :] += tile
                w_ref[rows, lanes] = tile.astype(jnp.bfloat16)
        acc[q] += jnp.dot(w_ref[...], images[k], preferred_element_type=f32)

    masses = columns_to_rows([jnp.sum(rsum[q], axis=1, keepdims=True) for q in range(n)])
    for q in range(n):
        src_out[q][:BLK, :] = acc[q]
        src_out[q][BLK:, :BLK] = jnp.broadcast_to(masses[q : q + 1, :], (8, BLK))
        src_out[q][BLK:, BLK:] = jnp.zeros((8, D - BLK), f32)


def src_norm_kernel(*refs):
    out = refs[-1]
    for h in range(2):
        own, plus, minus = refs[3 * h : 3 * h + 3]
        rows = slice(BLK, BLK + 8)
        mass = own[rows, :BLK] + plus[rows, :BLK] + minus[rows, :BLK]
        scale = to_columns(1.0 / mass)[:, :1]
        out[h * BLK : h * BLK + BLK, :] = (
            own[:BLK, :] + plus[:BLK, :] + minus[:BLK, :]
        ) * scale


def call(kernel, outs, args, smem, scratch=(), mib=50, hbm=(), flops=1 << 24):
    n = len(args)
    specs = [SMEM if i < smem else HBM if i in hbm else VMEM for i in range(n)]
    flat, tree = jax.tree.flatten(outs)
    out_specs = tree.unflatten([HBM if n + i in hbm else VMEM for i in range(len(flat))])
    return pl.pallas_call(
        kernel,
        out_shape=outs,
        in_specs=specs,
        out_specs=out_specs,
        scratch_shapes=list(scratch),
        compiler_params=pltpu.CompilerParams(vmem_limit_bytes=mib << 20),
        cost_estimate=pl.CostEstimate(
            flops=flops, bytes_accessed=8 << 20, transcendentals=CAP * BLK * BLK
        ),
    )(*args)


def sds(*shape):
    return jax.ShapeDtypeStruct(shape, f32)


def shift(a, axis, size, by):
    return lax.ppermute(a, axis, [(i, (i + by) % size) for i in range(size)])


def over_x(part):
    return [part] + [shift(part, "x", NX, k) for k in (1, 3, 2)]


def over_src(mine, give, join):
    got = shift(give, "c", NC, 1)
    both = join([mine, got])
    copies = jnp.broadcast_to(both[None], (NY * NZ, NB, 128))
    stack = lax.all_to_all(copies, ("y", "z"), 0, 0, tiled=True)
    return stack, shift(stack, "c", NC, 1)


def ring_scatter(own_a, own_b, plus_a, plus_b, far_a, far_b, minus_a, minus_b, axis, size):
    def move(value, by):
        return shift(value, axis, size, by)

    relay_up = move(far_a, 1)
    relay_down = move(far_b, -1)
    from_below_b = move(plus_b, 1)
    from_above_a = move(minus_a, -1)
    from_below_a = move(plus_a + relay_up, 1)
    from_above_b = move(minus_b + relay_down, -1)
    return (own_a, from_below_a, from_above_a), (own_b, from_below_b, from_above_b)


def program(text, image, log_mass_src, log_mass_tgt, pairs, count):
    mass_src = log_mass_src.reshape(NB, BLK)
    mass_tgt = log_mass_tgt.reshape(NB, BLK)
    pairs = pairs[:, 0] * NB + pairs[:, 1]
    place = jnp.stack([lax.axis_index(name) for name in ("x", "y", "c", "z")])
    row_scratch = [pltpu.VMEM((NB, BLK, 128), f32)] * 2
    col_scratch = [pltpu.VMEM((NB, BLK, 128), f32)] + [pltpu.VMEM((NB, 8, BLK), f32)] * 2
    tiles = [pltpu.VMEM((CAP, BLK, BLK), f32), pltpu.SemaphoreType.DMA((CAP,))]
    blocks = [pltpu.VMEM((NB, BLK, D), jnp.bfloat16)]
    block_sem = [pltpu.SemaphoreType.DMA((NB,))]
    stats = sds(NB, BLK)
    scores, part = call(
        first_kernel,
        (sds(CAP, BLK, BLK), stats),
        (count, pairs, text, image),
        2,
        row_scratch + tiles[:1] + blocks * 2 + tiles[1:] + block_sem * 2,
        52,
        (2, 3, 4),
        1 << 30,
    )
    lanes = sds(NB, 128)
    mine, give, u = call(
        col_kernel,
        (lanes, lanes, stats),
        (count, pairs, place, scores, *over_x(part), mass_src),
        3,
        col_scratch + tiles,
        hbm=(3,),
    )
    stack = over_src(mine, give, lse_of)
    plan, part = call(
        plan_kernel,
        (sds(CAP, BLK, BLK), stats),
        (count, pairs, place, scores, *stack, mass_tgt, u),
        3,
        [pltpu.VMEM((NB, BLK), f32)] + row_scratch + tiles + tiles[1:],
        hbm=(3, 8),
    )
    for _ in range(ITERS - 2):
        mine, give = call(
            col_sum_kernel,
            (lanes, lanes),
            (count, pairs, place, plan, *over_x(part), mass_src),
            3,
            [col_scratch[0], col_scratch[1]] + tiles,
            hbm=(3,),
        )
        stack = over_src(mine, give, sum)
        part = call(
            row_kernel,
            stats,
            (count, pairs, place, plan, *stack, mass_tgt),
            3,
            [pltpu.VMEM((NB, BLK), f32), row_scratch[0]] + tiles,
            hbm=(3,),
        )
    half = sds(NY, NZ, 32, D)
    mine, give, scale, keep, send = call(
        last_col_kernel,
        (lanes, lanes, stats, half, half),
        (count, pairs, place, plan, *over_x(part), mass_src, text),
        3,
        [col_scratch[0], col_scratch[1]]
        + tiles
        + blocks
        + block_sem
        + [pltpu.VMEM((BLK, BLK), jnp.bfloat16), pltpu.VMEM((NB, BLK, D), f32)],
        50,
        (3, 9),
        1 << 31,
    )
    got = shift(send, "c", NC, 1)
    stack = over_src(mine, give, sum)
    halves = call(add_kernel, tuple([sds(4, 32, D)] * 8), (keep, got), 0, (), 16)

    def final(offset, n):
        return call(
            functools.partial(final_kernel, offset, n),
            tuple([sds(BLK + 8, D)] * n),
            (count, pairs, place, plan, *stack, mass_tgt, scale, image),
            3,
            tiles
            + [
                pltpu.VMEM((CAP, BLK, D), jnp.bfloat16),
                tiles[1],
                pltpu.VMEM((NB, BLK), f32),
                pltpu.VMEM((NB, BLK), f32),
                pltpu.VMEM((n, BLK, 128), f32),
                pltpu.VMEM((BLK, BLK), jnp.bfloat16),
                pltpu.VMEM((n, BLK, D), f32),
                pltpu.VMEM((n, BLK, 128), f32),
            ],
            51,
            (3, 8),
            1 << 29,
        )

    far = final(4, 2)
    near = final(6, 6)
    part_a, part_b = ring_scatter(*near[2:], *far, *near[:2], "x", NX)
    tgt_a, tgt_b = ring_scatter(*halves, "y", NY)
    summed = jnp.concatenate([sum(tgt_a), sum(tgt_b)], axis=0)
    got = lax.all_to_all(summed, "z", 0, 0, tiled=True)
    tgt_map = call(
        tgt_norm_kernel, sds(32, D), (place, got, *stack), 1, [pltpu.VMEM((BLK, 128), f32)], 16
    )
    src_map = call(src_norm_kernel, sds(2 * BLK, D), (*part_a, *part_b), 0, (), 16)
    return (src_map, tgt_map)


def solution(mesh):
    grid = Mesh(mesh.devices.reshape(NY, NZ, NC, NX), ("y", "z", "c", "x"))
    src = ("y", "z", "c")
    return jax.shard_map(
        program,
        mesh=grid,
        in_specs=(P(src, None), P("x", None), P(src), P("x"), P((*src, "x"), None), P((*src, "x"))),
        out_specs=(P((*src, "x"), None), P(("x", *src), None)),
        check_vma=False,
    )
```
